256 devices in a mesh: depth: 32 (over z, x), tile: 8 (over y, core).
Axes of the slice: x: 4, y: 4, z: 8, core: 2. Of those that a mesh axis runs over, the one named last changes fastest.
Arguments:
- volume: bfloat16 [256, 512, 4096], P('depth', 'tile'), may hold values from -6 to 6
- shear: int32 [256], replicated, may hold values from -64 to 64, as said below
- footprint: int32 [32, 2], P('depth'), may hold values from 0 to 4096, as said below
Outputs:
- frame: float32 [4, 512, 4096], P(None, 'tile', 'depth')
The draws below stay inside these ranges and needn't reach their ends.
Inputs may be any that keep to these rules, and one draw needn't show every extreme that they name: Offsets follow a linear tilt over the slices with small jitter; shear[0] and shear[255] are the two ends of the range, in either order. footprint[b, 0] < 1024 and footprint[b, 1] > 3072 for every brick.
All inputs are finite; a program needn't handle non-finite values.
Results may differ from the reference program's by a relative error of at most 0.00085.
Values may be sent and summed in bfloat16 or wider, within the bound.
A program may use at most 64 MiB of HBM per device.

```python
import jax
import jax.numpy as jnp
from jax import lax

NY = 4096
DZ = 8
SMAX = 64
BRICKS = 32
NZ = 256
NX = 512


def draw_shear(key, part):
    first, second = jax.random.split(jax.random.fold_in(key, 11))
    sign = jax.random.randint(first, (), 0, 2) * 2 - 1
    slices = jnp.arange(NZ, dtype=jnp.int32)
    base = (2 * slices - NZ) * SMAX // NZ * sign
    jitter = jax.random.randint(second, (NZ,), -2, 3)
    offsets = jnp.clip(base + jitter, -SMAX, SMAX)
    offsets = offsets.at[0].set(-SMAX * sign).at[NZ - 1].set(SMAX * sign)
    return offsets.astype(jnp.int32)


def draw_footprint(key, part):
    first, second = jax.random.split(jax.random.fold_in(key, 23))
    count = NZ // DZ
    low = jax.random.randint(first, (count,), 0, NY // 4)
    high = NY - jax.random.randint(second, (count,), 0, NY // 4)
    low = low.at[0].set(0)
    high = high.at[count - 1].set(NY)
    return jnp.stack([low, high], axis=1).astype(jnp.int32)


def steps_of(rng, dims, cuts, least, high):
    def one(position, blocks):
        steps = jax.random.uniform(jax.random.fold_in(jax.random.fold_in(rng, 6), position), (blocks,), jnp.float32, least / len(cuts), high / len(cuts))
        return jnp.repeat(jnp.exp(steps), dims[position] // blocks).reshape((-1,) + (1,) * (len(dims) - position - 1))

    loudness = one(*cuts[0])
    for cut in cuts[1:]:
        loudness = loudness * one(*cut)
    return loudness


def bell_draw(rng, extent, spread, limit, shards=(), kind=jnp.bfloat16):
    result = spread * jax.random.normal(rng, extent, jnp.float32)
    if shards:
        result = result * steps_of(rng, extent, shards, -0.22, 0.18)
    return jnp.clip(result, -limit, limit).astype(kind)


def setup_inputs(seed: int = 0) -> dict:
    key_list = jax.random.split(jax.random.key(seed), 4)
    return {
        "volume": bell_draw(key_list[0], (NZ, NX, NY), 1.0, 6.0, ((0, 32), (1, 8))),
        "shear": draw_shear(jax.random.fold_in(key_list[3], 71), 0),
        "footprint": draw_footprint(jax.random.fold_in(key_list[3], 71), 0),
    }


def colour(cur, gx, gy, gz, offset, low, high, absorb):
    norm = jnp.sqrt(gx * gx + gy * gy + gz * gz + 1.0)
    shade = 0.3 + 0.7 * jnp.abs(0.48 * gx + 0.6 * gy + 0.64 * gz) / norm
    alpha = 1.0 - jnp.exp(-absorb * cur * cur)
    rgba = jnp.stack([shade * jax.nn.sigmoid(1.2 * cur + 0.2) * alpha, shade * jax.nn.sigmoid(-0.8 * cur) * alpha, shade * jax.nn.sigmoid(0.5 * cur - 0.3) * alpha, alpha])
    padded = jnp.pad(rgba, ((0, 0), (0, 0), (SMAX, SMAX)))
    moved = lax.dynamic_slice_in_dim(padded, (SMAX - offset).astype(jnp.int32), NY, 2)
    column = jnp.arange(NY, dtype=jnp.int32)
    inside = ((column >= low) & (column < high)).astype(jnp.float32)
    return moved * inside

def reference(volume, shear, footprint):
    flip = shear[0] > shear[NZ - 1]
    ascending = jnp.arange(BRICKS, dtype=jnp.int32)
    order = jnp.where(flip, BRICKS - 1 - ascending, ascending).astype(jnp.int32)
    absorb = 2.0 / NZ

    def brick_step(image, brick):

        def slice_step(acc, step):
            local = jnp.where(flip, DZ - 1 - step, step).astype(jnp.int32)
            index = (brick * DZ + local).astype(jnp.int32)
            cur = lax.dynamic_index_in_dim(volume, index, 0, keepdims=False).astype(jnp.float32)
            prev = lax.dynamic_index_in_dim(volume, jnp.maximum(index - 1, 0).astype(jnp.int32), 0, keepdims=False).astype(jnp.float32)
            nxt = lax.dynamic_index_in_dim(volume, jnp.minimum(index + 1, NZ - 1).astype(jnp.int32), 0, keepdims=False).astype(jnp.float32)
            prev = jnp.where(index > 0, prev, 0.0)
            nxt = jnp.where(index < NZ - 1, nxt, 0.0)
            gz = 0.5 * (nxt - prev)
            rows = jnp.pad(cur, ((1, 1), (0, 0)))
            gx = 0.5 * (rows[2:] - rows[:-2])
            cols = jnp.pad(cur, ((0, 0), (1, 1)))
            gy = 0.5 * (cols[:, 2:] - cols[:, :-2])
            placed = colour(cur, gx, gy, gz, shear[index], footprint[brick, 0], footprint[brick, 1], absorb)
            return (acc + (1.0 - acc[3:4]) * placed, None)
        acc, _ = lax.scan(slice_step, jnp.zeros((4, NX, NY), jnp.float32), jnp.arange(DZ, dtype=jnp.int32))
        partial_value = lax.optimization_barrier(acc.astype(jnp.bfloat16)).astype(jnp.float32)
        return (image + (1.0 - image[3:4]) * partial_value, None)
    frame, _ = lax.scan(brick_step, jnp.zeros((4, NX, NY), jnp.float32), order)
    return frame
```

```python
import functools
import math

import jax
import jax.numpy as jnp
from jax import lax
from jax.experimental import pallas as pl
from jax.experimental.pallas import tpu as pltpu
from jax.sharding import PartitionSpec as P

MESH = pl.DeviceIdType.MESH
LANES = 128
WIDE = 2 * LANES
HALO = 8
LAG = 2
TILE = 16


def kernel(
    groups,
    members,
    shear_ref,
    foot_ref,
    vol_ref,
    out_ref,
    slab,
    above,
    below,
    weights,
    fields,
    sent,
    got,
    staged,
    merged,
    load_sem,
    row_send,
    row_recv,
    halo_send,
    halo_recv,
    x_send,
    x_recv,
    z_send,
    z_recv,
):
    slices, rows, columns = vol_ref.shape
    bricks = groups * members
    total = slices * bricks
    tiles = lax.axis_size("tile")
    me, tile = lax.axis_index("depth"), lax.axis_index("tile")
    z, x = me // members, me % members
    span = members * LANES
    wide = members // 2
    tall = rows + 2 * HALO
    decay = -(2.0 / total) * math.log2(math.e)
    flip = shear_ref[0] > shear_ref[total - 1]

    def offset(k):
        half = groups // 2
        return half + k // 2 - (k % 2) * (2 * (k // 2) + 1)

    def owner(k):
        return (z + offset(k)) % groups

    following, leading = (me + 1) % bricks, (me + bricks - 1) % bricks
    lower, upper = (tile + 1) % tiles, (tile + tiles - 1) % tiles

    barrier = pltpu.get_barrier_semaphore()

    def greet(depth_id, tile_id):
        pl.semaphore_signal(
            barrier, inc=1, device_id=(depth_id, tile_id), device_id_type=MESH
        )

    for d in range(1, members):
        greet(z * members + (x + d) % members, tile)
    for d in range(1, groups):
        greet(((z + d) % groups) * members + x, tile)
    greet(following, tile)
    greet(leading, tile)
    greet(me, lower)
    greet(me, upper)

    load = pltpu.make_async_copy(
        vol_ref,
        slab.at[pl.ds(1, slices), pl.ds(0, rows), pl.ds(LANES, columns)],
        load_sem,
    )
    load.start()
    pl.semaphore_wait(barrier, members + groups + 2)

    def halo(k, up):
        peer = following if up else leading
        piece = (peer // members + offset(k)) % groups
        start = pl.multiple_of(piece * span, LANES)
        return pltpu.make_async_remote_copy(
            src_ref=vol_ref.at[slices - 1 if up else 0, :, pl.ds(start, span)],
            dst_ref=slab.at[
                0 if up else slices + 1,
                pl.ds(0, rows),
                pl.ds(pl.multiple_of(start + LANES, LANES), span),
            ],
            send_sem=halo_send.at[0 if up else 1, k],
            recv_sem=halo_recv.at[0 if up else 1, k],
            device_id=(peer, tile),
            device_id_type=MESH,
        )

    def row_halo(down):
        return pltpu.make_async_remote_copy(
            src_ref=vol_ref.at[:, pl.ds(rows - HALO if down else 0, HALO), :],
            dst_ref=above if down else below,
            send_sem=row_send.at[0 if down else 1],
            recv_sem=row_recv.at[0 if down else 1],
            device_id=(me, lower if down else upper),
            device_id_type=MESH,
        )

    row_halo(True).start()
    row_halo(False).start()

    def start_halo(k, carry):
        halo(k, True).start()
        halo(k, False).start()
        return carry

    lax.fori_loop(0, groups, start_halo, 0)

    slab[:, :, 0:LANES] = jnp.zeros((slices + 2, tall, LANES), slab.dtype)
    slab[:, :, pl.ds(LANES + columns, LANES)] = jnp.zeros(
        (slices + 2, tall, LANES), slab.dtype
    )

    def weigh(s, carry):
        shift = shear_ref[me * slices + s]
        lead = lax.broadcasted_iota(jnp.int32, (WIDE, WIDE), 0)
        lead = lead - lax.broadcasted_iota(jnp.int32, (WIDE, WIDE), 1)
        for part, base in ((0, LANES), (1, -LANES)):
            at = lead - (base - shift)
            weights[s, part] = jnp.where(at == 0, 1.0, 0.0).astype(weights.dtype)
            weights[s, 2 + part] = (
                jnp.where(at == 1, 1.0, jnp.where(at == -1, -1.0, 0.0))
            ).astype(weights.dtype)
        return carry

    lax.fori_loop(0, slices, weigh, 0)

    load.wait()
    row_halo(True).wait_recv()
    row_halo(False).wait_recv()

    def join_rows(s, carry):
        low = jnp.where(tile < tiles - 1, below[s].astype(jnp.float32), 0.0)
        high = jnp.where(tile > 0, above[s].astype(jnp.float32), 0.0)
        slab[1 + s, pl.ds(rows, 2 * HALO), pl.ds(LANES, columns)] = jnp.concatenate(
            [low, high], axis=0
        ).astype(slab.dtype)
        return carry

    lax.fori_loop(0, slices, join_rows, 0)

    def await_halo(k):
        halo(k, True).wait_recv()
        halo(k, False).wait_recv()
        start = pl.multiple_of(owner(k) * span + LANES, LANES)

        @pl.when(me == 0)
        def _():
            slab[0, pl.ds(0, rows), pl.ds(start, span)] = jnp.zeros(
                (rows, span), slab.dtype
            )

        @pl.when(me == bricks - 1)
        def _():
            slab[slices + 1, pl.ds(0, rows), pl.ds(start, span)] = jnp.zeros(
                (rows, span), slab.dtype
            )

    def shift_slice(s, start):
        def block(i, j, height):
            at = pl.multiple_of(start + j * WIDE, LANES)
            return slab[i, pl.ds(0, height), pl.ds(at, WIDE)]

        cur = [block(s + 1, j, tall) for j in range(wide + 1)]
        nxt = [block(s + 2, j, rows) for j in range(wide + 1)]
        prv = [block(s, j, rows) for j in range(wide + 1)]

        def through(blocks, which):
            low = jnp.concatenate([b for one in blocks for b in one[:-1]], axis=0)
            high = jnp.concatenate([b for one in blocks for b in one[1:]], axis=0)
            return jnp.dot(
                low, weights[s, which], preferred_element_type=jnp.float32
            ) + jnp.dot(
                high, weights[s, which + 1], preferred_element_type=jnp.float32
            )

        moved = through([cur, nxt, prv], 0)
        sloped = through([[b[:rows] for b in cur]], 2)
        for j in range(wide):
            strip = moved[j * tall : (j + 1) * tall]
            at = wide * tall + j * rows
            after = moved[at : at + rows]
            at = wide * (tall + rows) + j * rows
            before = moved[at : at + rows]
            down = pltpu.roll(strip, tall - 1, 0)[:rows]
            up = pltpu.roll(strip, 1, 0)[:rows]
            found = (
                strip[:rows],
                down - up,
                sloped[j * rows : (j + 1) * rows],
                after - before,
            )
            for q, value in enumerate(found):
                for h in range(2):
                    fields[q, s, 2 * j + h] = value[:, h * LANES : (h + 1) * LANES]

    def shade_tile(k, i):
        block, part = i // (rows // TILE), i % (rows // TILE)
        at = pl.ds(pl.multiple_of(part * TILE, TILE), TILE)
        shape = (TILE, LANES)
        left = jnp.ones(shape, jnp.float32)
        base = jnp.zeros(shape, jnp.float32)
        tint = [jnp.zeros(shape, jnp.float32)] * 3
        for step in range(slices):
            s = jnp.where(flip, slices - 1 - step, step)
            v = fields[0, s, block, at]
            dx = fields[1, s, block, at]
            dy = fields[2, s, block, at]
            dz = fields[3, s, block, at]
            facing = jnp.abs(
                (0.35 * 0.48) * dx + (0.35 * 0.6) * dy + (0.35 * 0.64) * dz
            )
            shade = 0.15 + facing * lax.rsqrt(dx * dx + dy * dy + dz * dz + 4.0)
            rest = left * jnp.exp2(decay * (v * v))
            weight = (left - rest) * shade
            left = rest
            base = base + weight
            turns = (
                jnp.tanh(0.6 * v + 0.1),
                jnp.tanh(-0.4 * v),
                jnp.tanh(0.25 * v - 0.15),
            )
            tint = [t + weight * turn for t, turn in zip(tint, turns)]
        first = (owner(k) * members + block) * LANES
        column = first + lax.broadcasted_iota(jnp.int32, shape, 1)
        inside = (column >= foot_ref[0, 0]) & (column < foot_ref[0, 1])
        for c, value in enumerate([base + t for t in tint] + [1.0 - left]):
            sent[k, block, c, at] = jnp.where(inside, value, 0.0).astype(sent.dtype)

    def exchange(k, d):
        peer = (x + d) % members
        return pltpu.make_async_remote_copy(
            src_ref=sent.at[k, peer],
            dst_ref=got.at[k, x],
            send_sem=x_send.at[k, d],
            recv_sem=x_recv.at[k, d],
            device_id=(z * members + peer, tile),
            device_id_type=MESH,
        )

    def hand_over(k):
        return pltpu.make_async_remote_copy(
            src_ref=staged.at[k],
            dst_ref=merged.at[z],
            send_sem=z_send.at[k],
            recv_sem=z_recv.at[k],
            device_id=(owner(k) * members + x, tile),
            device_id_type=MESH,
        )

    def merge(k, last):
        for d in range(1, members):
            exchange(k, d).wait_recv()
        got[k, x] = sent[k, x]

        def part(i, carry):
            at = pl.ds(pl.multiple_of(i * TILE, TILE), TILE)
            pieces = [
                [got[k, b, c, at].astype(jnp.float32) for c in range(4)]
                for b in range(members)
            ]
            for step in range(members):
                piece = [
                    jnp.where(flip, pieces[members - 1 - step][c], pieces[step][c])
                    for c in range(4)
                ]
                if step == 0:
                    colour, left = piece[:3], 1.0 - piece[3]
                else:
                    colour = [p + left * q for p, q in zip(colour, piece[:3])]
                    left = left * (1.0 - piece[3])
            for c, value in enumerate(colour + [left]):
                if last:
                    merged[z, c, at] = value
                else:
                    staged[k, c, at] = value
            return carry

        lax.fori_loop(0, rows // TILE, part, 0)
        if not last:
            hand_over(k).start()

    for k in range(2):
        await_halo(k)

    def advance(k, carry):
        @pl.when(k + 2 < groups)
        def _():
            await_halo(k + 2)

        start = owner(k) * span

        def one_slice(s, inner):
            shift_slice(s, start)
            return inner

        lax.fori_loop(0, slices, one_slice, 0)

        def one_tile(i, inner):
            shade_tile(k, i)
            return inner

        lax.fori_loop(0, members * (rows // TILE), one_tile, 0)
        for d in range(1, members):
            exchange(k, d).start()

        @pl.when(k >= LAG)
        def _():
            merge(k - LAG, False)

        return carry

    lax.fori_loop(0, groups, advance, 0)
    for k in range(groups - LAG, groups - 1):
        merge(k, False)
    merge(groups - 1, True)

    def arrive(k, carry):
        hand_over(k).wait_recv()
        return carry

    lax.fori_loop(0, groups - 1, arrive, 0)

    def finish(i, carry):
        at = pl.ds(pl.multiple_of(i * TILE, TILE), TILE)
        for step in range(groups):
            g = jnp.where(flip, groups - 1 - step, step)
            piece = [merged[g, c, at] for c in range(4)]
            if step == 0:
                colour, left = piece[:3], piece[3]
            else:
                colour = [p + left * q for p, q in zip(colour, piece[:3])]
                left = left * piece[3]
        for c, value in enumerate(colour + [1.0 - left]):
            out_ref[c, at] = value
        return carry

    lax.fori_loop(0, rows // TILE, finish, 0)

    row_halo(True).wait_send()
    row_halo(False).wait_send()

    def settle(k, carry):
        halo(k, True).wait_send()
        halo(k, False).wait_send()
        for d in range(1, members):
            exchange(k, d).wait_send()

        @pl.when(k < groups - 1)
        def _():
            hand_over(k).wait_send()

        return carry

    lax.fori_loop(0, groups, settle, 0)


def solution(mesh):
    members = 4
    groups = mesh.shape["depth"] // members

    def shards(volume, shear, footprint):
        slices, rows, columns = volume.shape
        tall = rows + 2 * HALO
        dma = pltpu.SemaphoreType.DMA
        return pl.pallas_call(
            functools.partial(kernel, groups, members),
            out_shape=jax.ShapeDtypeStruct((4, rows, LANES), jnp.float32),
            in_specs=[
                pl.BlockSpec(memory_space=pltpu.SMEM),
                pl.BlockSpec(memory_space=pltpu.SMEM),
                pl.BlockSpec(memory_space=pl.ANY),
            ],
            out_specs=pl.BlockSpec(memory_space=pltpu.VMEM),
            scratch_shapes=[
                pltpu.VMEM((slices + 2, tall, columns + 2 * LANES), jnp.bfloat16),
                pltpu.VMEM((slices, HALO, columns), jnp.bfloat16),
                pltpu.VMEM((slices, HALO, columns), jnp.bfloat16),
                pltpu.VMEM((slices, 4, WIDE, WIDE), jnp.bfloat16),
                pltpu.VMEM((4, slices, members, rows, LANES), jnp.float32),
                pltpu.VMEM((groups, members, 4, rows, LANES), jnp.bfloat16),
                pltpu.VMEM((groups, members, 4, rows, LANES), jnp.bfloat16),
                pltpu.VMEM((groups, 4, rows, LANES), jnp.float32),
                pltpu.VMEM((groups, 4, rows, LANES), jnp.float32),
                dma,
                dma((2,)),
                dma((2,)),
                dma((2, groups)),
                dma((2, groups)),
                dma((groups, members)),
                dma((groups, members)),
                dma((groups,)),
                dma((groups,)),
            ],
            compiler_params=pltpu.CompilerParams(
                collective_id=0,
                has_side_effects=True,
                vmem_limit_bytes=48 * 2**20,
            ),
        )(shear, footprint, volume)

    return jax.shard_map(
        shards,
        mesh=mesh,
        in_specs=(P("depth", "tile", None), P(), P("depth", None)),
        out_specs=P(None, "tile", "depth"),
        check_vma=False,
    )
```

```python
import functools
import math

import jax
import jax.numpy as jnp
from jax import lax
from jax.experimental import pallas as pl
from jax.experimental.pallas import tpu as pltpu
from jax.sharding import PartitionSpec as P

MESH = pl.DeviceIdType.MESH
LANES = 128
WIDE = 2 * LANES
HALO = 8
LAG = 2
TILE = 16


def kernel(
    groups,
    members,
    shear_hbm,
    foot_hbm,
    vol_ref,
    out_ref,
    shear_ref,
    foot_ref,
    slab,
    above,
    below,
    weights,
    fields,
    sent,
    got,
    staged,
    merged,
    load_sem,
    table_sem,
    row_send,
    row_recv,
    halo_send,
    halo_recv,
    x_send,
    x_recv,
    z_send,
    z_recv,
):
    slices, rows, columns = vol_ref.shape
    bricks = groups * members
    total = slices * bricks
    tiles = lax.axis_size("tile")
    me, tile = lax.axis_index("depth"), lax.axis_index("tile")
    z, x = me // members, me % members
    span = members * LANES
    wide = members // 2
    tall = rows + 2 * HALO
    decay = -(2.0 / total) * math.log2(math.e)

    def offset(k):
        half = groups // 2
        return half + k // 2 - (k % 2) * (2 * (k // 2) + 1)

    def owner(k):
        return (z + offset(k)) % groups

    following, leading = (me + 1) % bricks, (me + bricks - 1) % bricks
    lower, upper = (tile + 1) % tiles, (tile + tiles - 1) % tiles

    barrier = pltpu.get_barrier_semaphore()

    def greet(depth_id, tile_id):
        pl.semaphore_signal(
            barrier, inc=1, device_id=(depth_id, tile_id), device_id_type=MESH
        )

    for d in range(1, members):
        greet(z * members + (x + d) % members, tile)
    for d in range(1, groups):
        greet(((z + d) % groups) * members + x, tile)
    greet(following, tile)
    greet(leading, tile)
    greet(me, lower)
    greet(me, upper)

    load = pltpu.make_async_copy(
        vol_ref,
        slab.at[pl.ds(1, slices), pl.ds(0, rows), pl.ds(LANES, columns)],
        load_sem,
    )
    tables = [
        pltpu.make_async_copy(shear_hbm, shear_ref, table_sem.at[0]),
        pltpu.make_async_copy(foot_hbm, foot_ref, table_sem.at[1]),
    ]
    for table in tables:
        table.start()
    load.start()
    pl.semaphore_wait(barrier, members + groups + 2)

    def halo(k, up):
        peer = following if up else leading
        piece = (peer // members + offset(k)) % groups
        start = pl.multiple_of(piece * span, LANES)
        return pltpu.make_async_remote_copy(
            src_ref=vol_ref.at[slices - 1 if up else 0, :, pl.ds(start, span)],
            dst_ref=slab.at[
                0 if up else slices + 1,
                pl.ds(0, rows),
                pl.ds(pl.multiple_of(start + LANES, LANES), span),
            ],
            send_sem=halo_send.at[0 if up else 1, k],
            recv_sem=halo_recv.at[0 if up else 1, k],
            device_id=(peer, tile),
            device_id_type=MESH,
        )

    def row_halo(down):
        return pltpu.make_async_remote_copy(
            src_ref=vol_ref.at[:, pl.ds(rows - HALO if down else 0, HALO), :],
            dst_ref=above if down else below,
            send_sem=row_send.at[0 if down else 1],
            recv_sem=row_recv.at[0 if down else 1],
            device_id=(me, lower if down else upper),
            device_id_type=MESH,
        )

    row_halo(True).start()
    row_halo(False).start()

    def start_halo(k, carry):
        halo(k, True).start()
        halo(k, False).start()
        return carry

    lax.fori_loop(0, groups, start_halo, 0)

    slab[:, :, 0:LANES] = jnp.zeros((slices + 2, tall, LANES), slab.dtype)
    slab[:, :, pl.ds(LANES + columns, LANES)] = jnp.zeros(
        (slices + 2, tall, LANES), slab.dtype
    )

    for table in tables:
        table.wait()
    flip = shear_ref[0] > shear_ref[total - 1]

    def weigh(s, carry):
        shift = shear_ref[me * slices + s]
        lead = lax.broadcasted_iota(jnp.int32, (WIDE, WIDE), 0)
        lead = lead - lax.broadcasted_iota(jnp.int32, (WIDE, WIDE), 1)
        for part, base in ((0, LANES), (1, -LANES)):
            at = lead - (base - shift)
            rows_at = pl.ds(part * WIDE, WIDE)
            weights[s, 0, rows_at] = jnp.where(at == 0, 1.0, 0.0).astype(weights.dtype)
            weights[s, 1, rows_at] = jnp.where(
                at == 1, 1.0, jnp.where(at == -1, -1.0, 0.0)
            ).astype(weights.dtype)
        return carry

    lax.fori_loop(0, slices, weigh, 0)

    load.wait()
    row_halo(True).wait_recv()
    row_halo(False).wait_recv()

    def join_rows(s, carry):
        low = jnp.where(tile < tiles - 1, below[s].astype(jnp.float32), 0.0)
        high = jnp.where(tile > 0, above[s].astype(jnp.float32), 0.0)
        slab[1 + s, pl.ds(rows, 2 * HALO), pl.ds(LANES, columns)] = jnp.concatenate(
            [low, high], axis=0
        ).astype(slab.dtype)
        return carry

    lax.fori_loop(0, slices, join_rows, 0)

    def await_halo(k):
        halo(k, True).wait_recv()
        halo(k, False).wait_recv()
        start = pl.multiple_of(owner(k) * span + LANES, LANES)

        @pl.when(me == 0)
        def _():
            slab[0, pl.ds(0, rows), pl.ds(start, span)] = jnp.zeros(
                (rows, span), slab.dtype
            )

        @pl.when(me == bricks - 1)
        def _():
            slab[slices + 1, pl.ds(0, rows), pl.ds(start, span)] = jnp.zeros(
                (rows, span), slab.dtype
            )

    def shift_slice(s, start):
        def block(i, j, height):
            at = pl.multiple_of(start + j * WIDE, LANES)
            return slab[i, pl.ds(0, height), pl.ds(at, 2 * WIDE)]

        cur = [block(s + 1, j, tall) for j in range(wide)]
        nxt = [block(s + 2, j, rows) for j in range(wide)]
        prv = [block(s, j, rows) for j in range(wide)]

        def through(blocks, which):
            return jnp.dot(
                jnp.concatenate(blocks, axis=0),
                weights[s, which],
                preferred_element_type=jnp.float32,
            )

        moved = through(cur + nxt + prv, 0)
        sloped = through([b[:rows] for b in cur], 1)
        for j in range(wide):
            strip = moved[j * tall : (j + 1) * tall]
            at = wide * tall + j * rows
            after = moved[at : at + rows]
            at = wide * (tall + rows) + j * rows
            before = moved[at : at + rows]
            down = pltpu.roll(strip, tall - 1, 0)[:rows]
            up = pltpu.roll(strip, 1, 0)[:rows]
            found = (
                strip[:rows],
                down - up,
                sloped[j * rows : (j + 1) * rows],
                after - before,
            )
            for q, value in enumerate(found):
                for h in range(2):
                    fields[q, s, 2 * j + h] = value[:, h * LANES : (h + 1) * LANES]

    def shade_tile(k, i):
        block, part = i // (rows // TILE), i % (rows // TILE)
        at = pl.ds(pl.multiple_of(part * TILE, TILE), TILE)
        shape = (TILE, LANES)
        left = jnp.ones(shape, jnp.float32)
        base = jnp.zeros(shape, jnp.float32)
        tint = [jnp.zeros(shape, jnp.float32)] * 3
        for step in range(slices):
            s = jnp.where(flip, slices - 1 - step, step)
            v = fields[0, s, block, at]
            dx = fields[1, s, block, at]
            dy = fields[2, s, block, at]
            dz = fields[3, s, block, at]
            facing = jnp.abs(
                (0.35 * 0.48) * dx + (0.35 * 0.6) * dy + (0.35 * 0.64) * dz
            )
            shade = 0.15 + facing * lax.rsqrt(dx * dx + dy * dy + dz * dz + 4.0)
            rest = left * jnp.exp2(decay * (v * v))
            weight = (left - rest) * shade
            left = rest
            base = base + weight
            turns = (
                jnp.tanh(0.6 * v + 0.1),
                jnp.tanh(-0.4 * v),
                jnp.tanh(0.25 * v - 0.15),
            )
            tint = [t + weight * turn for t, turn in zip(tint, turns)]
        first = (owner(k) * members + block) * LANES
        column = first + lax.broadcasted_iota(jnp.int32, shape, 1)
        inside = (column >= foot_ref[0, 0]) & (column < foot_ref[0, 1])
        for c, value in enumerate([base + t for t in tint] + [1.0 - left]):
            sent[k, block, c, at] = jnp.where(inside, value, 0.0).astype(sent.dtype)

    def exchange(k, d):
        peer = (x + d) % members
        return pltpu.make_async_remote_copy(
            src_ref=sent.at[k, peer],
            dst_ref=got.at[k, x],
            send_sem=x_send.at[k, d],
            recv_sem=x_recv.at[k, d],
            device_id=(z * members + peer, tile),
            device_id_type=MESH,
        )

    def hand_over(k):
        return pltpu.make_async_remote_copy(
            src_ref=staged.at[k],
            dst_ref=merged.at[z],
            send_sem=z_send.at[k],
            recv_sem=z_recv.at[k],
            device_id=(owner(k) * members + x, tile),
            device_id_type=MESH,
        )

    def merge(k, last):
        for d in range(1, members):
            exchange(k, d).wait_recv()
        got[k, x] = sent[k, x]

        def part(i, carry):
            at = pl.ds(pl.multiple_of(i * TILE, TILE), TILE)
            pieces = [
                [got[k, b, c, at].astype(jnp.float32) for c in range(4)]
                for b in range(members)
            ]
            for step in range(members):
                piece = [
                    jnp.where(flip, pieces[members - 1 - step][c], pieces[step][c])
                    for c in range(4)
                ]
                if step == 0:
                    colour, left = piece[:3], 1.0 - piece[3]
                else:
                    colour = [p + left * q for p, q in zip(colour, piece[:3])]
                    left = left * (1.0 - piece[3])
            for c, value in enumerate(colour + [left]):
                if last:
                    merged[z, c, at] = value
                else:
                    staged[k, c, at] = value
            return carry

        lax.fori_loop(0, rows // TILE, part, 0)
        if not last:
            hand_over(k).start()

    for k in range(2):
        await_halo(k)

    def advance(k, carry):
        @pl.when(k + 2 < groups)
        def _():
            await_halo(k + 2)

        start = owner(k) * span

        def one_slice(s, inner):
            shift_slice(s, start)
            return inner

        lax.fori_loop(0, slices, one_slice, 0, unroll=8)

        def one_tile(i, inner):
            shade_tile(k, i)
            return inner

        lax.fori_loop(0, members * (rows // TILE), one_tile, 0, unroll=2)
        for d in range(1, members):
            exchange(k, d).start()

        @pl.when(k >= LAG)
        def _():
            merge(k - LAG, False)

        return carry

    lax.fori_loop(0, groups, advance, 0)
    for k in range(groups - LAG, groups - 1):
        merge(k, False)
    merge(groups - 1, True)

    def arrive(k, carry):
        hand_over(k).wait_recv()
        return carry

    lax.fori_loop(0, groups - 1, arrive, 0)

    def finish(i, carry):
        at = pl.ds(pl.multiple_of(i * TILE, TILE), TILE)
        for step in range(groups):
            g = jnp.where(flip, groups - 1 - step, step)
            piece = [merged[g, c, at] for c in range(4)]
            if step == 0:
                colour, left = piece[:3], piece[3]
            else:
                colour = [p + left * q for p, q in zip(colour, piece[:3])]
                left = left * piece[3]
        for c, value in enumerate(colour + [1.0 - left]):
            out_ref[c, at] = value
        return carry

    lax.fori_loop(0, rows // TILE, finish, 0)

    row_halo(True).wait_send()
    row_halo(False).wait_send()

    def settle(k, carry):
        halo(k, True).wait_send()
        halo(k, False).wait_send()
        for d in range(1, members):
            exchange(k, d).wait_send()

        @pl.when(k < groups - 1)
        def _():
            hand_over(k).wait_send()

        return carry

    lax.fori_loop(0, groups, settle, 0)


def solution(mesh):
    members = 4
    groups = mesh.shape["depth"] // members

    def shards(volume, shear, footprint):
        slices, rows, columns = volume.shape
        tall = rows + 2 * HALO
        dma = pltpu.SemaphoreType.DMA
        return pl.pallas_call(
            functools.partial(kernel, groups, members),
            out_shape=jax.ShapeDtypeStruct((4, rows, LANES), jnp.float32),
            in_specs=[
                pl.BlockSpec(memory_space=pltpu.HBM),
                pl.BlockSpec(memory_space=pltpu.HBM),
                pl.BlockSpec(memory_space=pltpu.HBM),
            ],
            out_specs=pl.BlockSpec(memory_space=pltpu.VMEM),
            scratch_shapes=[
                pltpu.SMEM(shear.shape, jnp.int32),
                pltpu.SMEM(footprint.shape, jnp.int32),
                pltpu.VMEM((slices + 2, tall, columns + 2 * LANES), jnp.bfloat16),
                pltpu.VMEM((slices, HALO, columns), jnp.bfloat16),
                pltpu.VMEM((slices, HALO, columns), jnp.bfloat16),
                pltpu.VMEM((slices, 2, 2 * WIDE, WIDE), jnp.bfloat16),
                pltpu.VMEM((4, slices, members, rows, LANES), jnp.float32),
                pltpu.VMEM((groups, members, 4, rows, LANES), jnp.bfloat16),
                pltpu.VMEM((groups, members, 4, rows, LANES), jnp.bfloat16),
                pltpu.VMEM((groups, 4, rows, LANES), jnp.float32),
                pltpu.VMEM((groups, 4, rows, LANES), jnp.float32),
                dma,
                dma((2,)),
                dma((2,)),
                dma((2,)),
                dma((2, groups)),
                dma((2, groups)),
                dma((groups, members)),
                dma((groups, members)),
                dma((groups,)),
                dma((groups,)),
            ],
            compiler_params=pltpu.CompilerParams(
                collective_id=0,
                has_side_effects=True,
                vmem_limit_bytes=48 * 2**20,
            ),
        )(*(pltpu.with_memory_space_constraint(a, pltpu.HBM) for a in (shear, footprint, volume)))

    return jax.shard_map(
        shards,
        mesh=mesh,
        in_specs=(P("depth", "tile", None), P(), P("depth", None)),
        out_specs=P(None, "tile", "depth"),
        check_vma=False,
    )
```

```python
import functools
import math

import jax
import jax.numpy as jnp
from jax import lax
from jax.experimental import pallas as pl
from jax.experimental.pallas import tpu as pltpu
from jax.sharding import PartitionSpec as P

MESH = pl.DeviceIdType.MESH
LANES = 128
WIDE = 2 * LANES
HALO = 8
LAG = 2
TILE = 16
UNROLL = 2
SPREAD = 200.0


def kernel(
    groups,
    members,
    shear_hbm,
    foot_hbm,
    vol_ref,
    out_ref,
    shear_ref,
    foot_ref,
    slab,
    above,
    below,
    weights,
    fields_even,
    fields_odd,
    sent,
    got,
    staged,
    merged,
    load_sem,
    table_sem,
    row_send,
    row_recv,
    halo_send,
    halo_recv,
    x_send,
    x_recv,
    z_send,
    z_recv,
):
    slices, rows, columns = vol_ref.shape
    bricks = groups * members
    total = slices * bricks
    tiles = lax.axis_size("tile")
    me, tile = lax.axis_index("depth"), lax.axis_index("tile")
    z, x = me // members, me % members
    span = members * LANES
    wide = members // 2
    tall = rows + 2 * HALO
    decay = -(2.0 / total) * math.log2(math.e)

    def offset(k):
        half = groups // 2
        return half + k // 2 - (k % 2) * (2 * (k // 2) + 1)

    def owner(k):
        return (z + offset(k)) % groups

    following, leading = (me + 1) % bricks, (me + bricks - 1) % bricks
    lower, upper = (tile + 1) % tiles, (tile + tiles - 1) % tiles

    barrier = pltpu.get_barrier_semaphore()

    def greet(depth_id, tile_id):
        pl.semaphore_signal(
            barrier, inc=1, device_id=(depth_id, tile_id), device_id_type=MESH
        )

    for d in range(1, members):
        greet(z * members + (x + d) % members, tile)
    for d in range(1, groups):
        greet(((z + d) % groups) * members + x, tile)
    greet(following, tile)
    greet(leading, tile)
    greet(me, lower)
    greet(me, upper)

    load = pltpu.make_async_copy(
        vol_ref,
        slab.at[pl.ds(1, slices), pl.ds(0, rows), pl.ds(LANES, columns)],
        load_sem,
    )
    tables = [
        pltpu.make_async_copy(shear_hbm, shear_ref, table_sem.at[0]),
        pltpu.make_async_copy(foot_hbm, foot_ref, table_sem.at[1]),
    ]
    for table in tables:
        table.start()
    load.start()
    pl.semaphore_wait(barrier, members + groups + 2)

    def block_of(depth_id, u, h):
        first = 2 * (depth_id // members) + groups
        away = (u % 2) * (2 * u + 1) - u - 1
        blocks = 2 * groups
        return ((first + away + h + blocks) % blocks) * WIDE

    def halo(u, h, up):
        peer = following if up else leading
        start = pl.multiple_of(block_of(peer, u, h), LANES)
        return pltpu.make_async_remote_copy(
            src_ref=vol_ref.at[slices - 1 if up else 0, :, pl.ds(start, WIDE)],
            dst_ref=slab.at[
                0 if up else slices + 1,
                pl.ds(0, rows),
                pl.ds(pl.multiple_of(start + LANES, LANES), WIDE),
            ],
            send_sem=halo_send.at[0 if up else 1, u, h],
            recv_sem=halo_recv.at[0 if up else 1, u, h],
            device_id=(peer, tile),
            device_id_type=MESH,
        )

    def row_halo(u, h, down):
        at = pl.ds(pl.multiple_of(block_of(me, u, h), LANES), WIDE)
        edge = pl.ds(rows - HALO if down else 0, HALO)
        return pltpu.make_async_remote_copy(
            src_ref=vol_ref.at[:, edge, at],
            dst_ref=(above if down else below).at[:, :, at],
            send_sem=row_send.at[0 if down else 1, u, h],
            recv_sem=row_recv.at[0 if down else 1, u, h],
            device_id=(me, lower if down else upper),
            device_id_type=MESH,
        )

    def start_halo(u, carry):
        for h in range(2):
            halo(u, h, True).start()
            halo(u, h, False).start()
            row_halo(u, h, True).start()
            row_halo(u, h, False).start()
        return carry

    lax.fori_loop(0, groups, start_halo, 0)

    slab[:, :, 0:LANES] = jnp.zeros((slices + 2, tall, LANES), slab.dtype)
    slab[:, :, pl.ds(LANES + columns, LANES)] = jnp.zeros(
        (slices + 2, tall, LANES), slab.dtype
    )

    for table in tables:
        table.wait()
    flip = shear_ref[0] > shear_ref[total - 1]

    def weigh(s, carry):
        shift = shear_ref[me * slices + s]
        lead = lax.broadcasted_iota(jnp.int32, (WIDE, WIDE), 0)
        lead = lead - lax.broadcasted_iota(jnp.int32, (WIDE, WIDE), 1)
        for part, base in ((0, LANES), (1, -LANES)):
            at = lead - (base - shift)
            rows_at = pl.ds(part * WIDE, WIDE)
            weights[s, 0, rows_at] = jnp.where(at == 0, 1.0, 0.0).astype(weights.dtype)
            weights[s, 1, rows_at] = jnp.where(
                at == 1, 1.0, jnp.where(at == -1, -1.0, 0.0)
            ).astype(weights.dtype)
        return carry

    lax.fori_loop(0, slices, weigh, 0)

    load.wait()

    def await_rows(u):
        for h in range(2):
            row_halo(u, h, True).wait_recv()
            row_halo(u, h, False).wait_recv()
            start = pl.multiple_of(block_of(me, u, h), LANES)
            at = pl.ds(start, WIDE)
            low = jnp.where(tile < tiles - 1, below[:, :, at].astype(jnp.float32), 0.0)
            high = jnp.where(tile > 0, above[:, :, at].astype(jnp.float32), 0.0)
            at = pl.ds(pl.multiple_of(start + LANES, LANES), WIDE)
            slab[pl.ds(1, slices), pl.ds(rows, 2 * HALO), at] = jnp.concatenate(
                [low, high], axis=1
            ).astype(slab.dtype)

    def await_depth(u):
        for h in range(2):
            halo(u, h, True).wait_recv()
            halo(u, h, False).wait_recv()
            start = pl.multiple_of(block_of(me, u, h) + LANES, LANES)
            at = pl.ds(start, WIDE)

            @pl.when(me == 0)
            def _():
                slab[0, pl.ds(0, rows), at] = jnp.zeros((rows, WIDE), slab.dtype)

            @pl.when(me == bricks - 1)
            def _():
                slab[slices + 1, pl.ds(0, rows), at] = jnp.zeros(
                    (rows, WIDE), slab.dtype
                )

    def shift_slice(s, start, fields):
        def block(i, j, height):
            at = pl.multiple_of(start + j * WIDE, LANES)
            return slab[i, pl.ds(0, height), pl.ds(at, 2 * WIDE)]

        cur = [block(s + 1, j, tall) for j in range(wide)]
        nxt = [block(s + 2, j, rows) for j in range(wide)]
        prv = [block(s, j, rows) for j in range(wide)]

        def through(blocks, which):
            return jnp.dot(
                jnp.concatenate(blocks, axis=0),
                weights[s, which],
                preferred_element_type=jnp.float32,
            )

        moved = through(cur + nxt + prv, 0)
        sloped = through([b[:rows] for b in cur], 1)
        for j in range(wide):
            strip = moved[j * tall : (j + 1) * tall]
            at = wide * tall + j * rows
            after = moved[at : at + rows]
            at = wide * (tall + rows) + j * rows
            before = moved[at : at + rows]
            down = pltpu.roll(strip, tall - 1, 0)[:rows]
            up = pltpu.roll(strip, 1, 0)[:rows]
            found = (
                strip[:rows],
                down - up,
                sloped[j * rows : (j + 1) * rows],
                after - before,
            )
            for q, value in enumerate(found):
                for h in range(2):
                    fields[q, s, 2 * j + h] = value[:, h * LANES : (h + 1) * LANES]

    def shade_tile(k, i, fields):
        block, part = i // (rows // TILE), i % (rows // TILE)
        at = pl.ds(pl.multiple_of(part * TILE, TILE), TILE)
        shape = (TILE, LANES)
        left = jnp.ones(shape, jnp.float32)
        base = jnp.zeros(shape, jnp.float32)
        tint = [jnp.zeros(shape, jnp.float32)] * 3
        for step in range(slices):
            s = jnp.where(flip, slices - 1 - step, step)
            v = fields[0, s, block, at]
            dx = fields[1, s, block, at]
            dy = fields[2, s, block, at]
            dz = fields[3, s, block, at]
            facing = jnp.abs(
                (0.35 * 0.48) * dx + (0.35 * 0.6) * dy + (0.35 * 0.64) * dz
            )
            shade = 0.15 + facing * lax.rsqrt(dx * dx + dy * dy + dz * dz + 4.0)
            rest = left * jnp.exp2(decay * (v * v))
            weight = (left - rest) * shade
            left = rest
            base = base + weight
            turns = (
                jnp.tanh(0.6 * v + 0.1),
                jnp.tanh(-0.4 * v),
                jnp.tanh(0.25 * v - 0.15),
            )
            tint = [t + weight * turn for t, turn in zip(tint, turns)]
        first = (owner(k) * members + block) * LANES
        column = first + lax.broadcasted_iota(jnp.int32, shape, 1)
        inside = (column >= foot_ref[0, 0]) & (column < foot_ref[0, 1])
        for c, value in enumerate([base + t for t in tint] + [1.0 - left]):
            sent[k, block, c, at] = jnp.where(inside, value, 0.0).astype(sent.dtype)

    def exchange(k, d):
        peer = (x + d) % members
        return pltpu.make_async_remote_copy(
            src_ref=sent.at[k, peer],
            dst_ref=got.at[k, x],
            send_sem=x_send.at[k, d],
            recv_sem=x_recv.at[k, d],
            device_id=(z * members + peer, tile),
            device_id_type=MESH,
        )

    def hand_over(k):
        return pltpu.make_async_remote_copy(
            src_ref=staged.at[k],
            dst_ref=merged.at[z],
            send_sem=z_send.at[k],
            recv_sem=z_recv.at[k],
            device_id=(owner(k) * members + x, tile),
            device_id_type=MESH,
        )

    def spread(value):
        return jnp.exp2(SPREAD * (value - 0.5))

    def gather(code):
        return jnp.log2(code) * (1.0 / SPREAD) + 0.5

    def merge(k, last):
        for d in range(1, members):
            exchange(k, d).wait_recv()
        got[k, x] = sent[k, x]

        def part(i, carry):
            at = pl.ds(pl.multiple_of(i * TILE, TILE), TILE)
            pieces = [
                [got[k, b, c, at].astype(jnp.float32) for c in range(4)]
                for b in range(members)
            ]
            for step in range(members):
                piece = [
                    jnp.where(flip, pieces[members - 1 - step][c], pieces[step][c])
                    for c in range(4)
                ]
                if step == 0:
                    colour, left = piece[:3], 1.0 - piece[3]
                else:
                    colour = [p + left * q for p, q in zip(colour, piece[:3])]
                    left = left * (1.0 - piece[3])
            for c, value in enumerate(colour + [left]):
                if last:
                    merged[z, c, at] = spread(value).astype(merged.dtype)
                else:
                    staged[k, c, at] = spread(value).astype(staged.dtype)
            return carry

        lax.fori_loop(0, rows // TILE, part, 0)
        if not last:
            hand_over(k).start()

    each = members * (rows // TILE) // slices

    def shade_only(k, fields):
        def body(i, carry):
            for t in range(each):
                shade_tile(k, i * each + t, fields)
            return carry

        lax.fori_loop(0, slices, body, 0)

    def shade_and_shift(k, fields, ahead):
        start = owner(k + 1) * span

        def body(i, carry):
            shift_slice(i, start, ahead)
            for t in range(each):
                shade_tile(k, i * each + t, fields)
            return carry

        lax.fori_loop(0, slices, body, 0, unroll=UNROLL)

    def pass_on(k):
        for d in range(1, members):
            exchange(k, d).start()

        @pl.when(k >= LAG)
        def _():
            merge(k - LAG, False)

    await_rows(0)
    await_rows(1)
    first = owner(0) * span

    def inner(s, carry):
        shift_slice(s, first, fields_even)
        return carry

    lax.fori_loop(1, slices - 1, inner, 0, unroll=(slices - 2) // 2)
    await_depth(0)
    await_depth(1)
    shift_slice(0, first, fields_even)
    shift_slice(slices - 1, first, fields_even)

    def advance(h, carry):
        for part, fields, ahead in (
            (0, fields_even, fields_odd),
            (1, fields_odd, fields_even),
        ):
            k = 2 * h + part
            await_rows(k + 2)
            await_depth(k + 2)
            shade_and_shift(k, fields, ahead)
            pass_on(k)
        return carry

    lax.fori_loop(0, groups // 2 - 1, advance, 0)
    shade_and_shift(groups - 2, fields_even, fields_odd)
    pass_on(groups - 2)
    shade_only(groups - 1, fields_odd)
    pass_on(groups - 1)
    for k in range(groups - LAG, groups - 1):
        merge(k, False)
    merge(groups - 1, True)

    def arrive(k, carry):
        hand_over(k).wait_recv()
        return carry

    lax.fori_loop(0, groups - 1, arrive, 0)

    def finish(i, carry):
        at = pl.ds(pl.multiple_of(i * TILE, TILE), TILE)
        for step in range(groups):
            g = jnp.where(flip, groups - 1 - step, step)
            piece = [gather(merged[g, c, at].astype(jnp.float32)) for c in range(4)]
            if step == 0:
                colour, left = piece[:3], piece[3]
            else:
                colour = [p + left * q for p, q in zip(colour, piece[:3])]
                left = left * piece[3]
        for c, value in enumerate(colour + [1.0 - left]):
            out_ref[c, at] = value
        return carry

    lax.fori_loop(0, rows // TILE, finish, 0)

    def settle(k, carry):
        for h in range(2):
            halo(k, h, True).wait_send()
            halo(k, h, False).wait_send()
            row_halo(k, h, True).wait_send()
            row_halo(k, h, False).wait_send()
        for d in range(1, members):
            exchange(k, d).wait_send()

        @pl.when(k < groups - 1)
        def _():
            hand_over(k).wait_send()

        return carry

    lax.fori_loop(0, groups, settle, 0)


def solution(mesh):
    members = 4
    groups = mesh.shape["depth"] // members

    def shards(volume, shear, footprint):
        slices, rows, columns = volume.shape
        tall = rows + 2 * HALO
        dma = pltpu.SemaphoreType.DMA
        return pl.pallas_call(
            functools.partial(kernel, groups, members),
            out_shape=jax.ShapeDtypeStruct((4, rows, LANES), jnp.float32),
            in_specs=[
                pl.BlockSpec(memory_space=pltpu.HBM),
                pl.BlockSpec(memory_space=pltpu.HBM),
                pl.BlockSpec(memory_space=pltpu.HBM),
            ],
            out_specs=pl.BlockSpec(memory_space=pltpu.VMEM),
            scratch_shapes=[
                pltpu.SMEM(shear.shape, jnp.int32),
                pltpu.SMEM(footprint.shape, jnp.int32),
                pltpu.VMEM((slices + 2, tall, columns + 2 * LANES), jnp.bfloat16),
                pltpu.VMEM((slices, HALO, columns), jnp.bfloat16),
                pltpu.VMEM((slices, HALO, columns), jnp.bfloat16),
                pltpu.VMEM((slices, 2, 2 * WIDE, WIDE), jnp.bfloat16),
                pltpu.VMEM((4, slices, members, rows, LANES), jnp.float32),
                pltpu.VMEM((4, slices, members, rows, LANES), jnp.float32),
                pltpu.VMEM((groups, members, 4, rows, LANES), jnp.bfloat16),
                pltpu.VMEM((groups, members, 4, rows, LANES), jnp.bfloat16),
                pltpu.VMEM((groups, 4, rows, LANES), jnp.bfloat16),
                pltpu.VMEM((groups, 4, rows, LANES), jnp.bfloat16),
                dma,
                dma((2,)),
                dma((2, groups, 2)),
                dma((2, groups, 2)),
                dma((2, groups, 2)),
                dma((2, groups, 2)),
                dma((groups, members)),
                dma((groups, members)),
                dma((groups,)),
                dma((groups,)),
            ],
            compiler_params=pltpu.CompilerParams(
                collective_id=0,
                has_side_effects=True,
                vmem_limit_bytes=48 * 2**20,
            ),
        )(*(pltpu.with_memory_space_constraint(a, pltpu.HBM) for a in (shear, footprint, volume)))

    return jax.shard_map(
        shards,
        mesh=mesh,
        in_specs=(P("depth", "tile", None), P(), P("depth", None)),
        out_specs=P(None, "tile", "depth"),
        check_vma=False,
    )
```

```python
import functools
import math

import jax
import jax.numpy as jnp
from jax import lax
from jax.experimental import pallas as pl
from jax.experimental.pallas import tpu as pltpu
from jax.sharding import PartitionSpec as P

MESH = pl.DeviceIdType.MESH
LANES = 128
WIDE = 2 * LANES
HALO = 8
LAG = 3
TILE = 16
UNROLL = 2
SPREAD = 200.0
ORDERS = (
    (4, 5, 6, 7, 1, 2, 3, 0),
    (5, 6, 7, 4, 0, 2, 3, 1),
    (6, 7, 4, 5, 0, 1, 3, 2),
    (0, 1, 2, 7, 6, 5, 4, 3),
    (0, 1, 2, 3, 5, 6, 7, 4),
    (1, 2, 3, 0, 6, 7, 4, 5),
    (2, 3, 0, 1, 7, 4, 5, 6),
    (3, 0, 1, 2, 4, 5, 6, 7),
)


def kernel(
    groups,
    members,
    shear_hbm,
    foot_hbm,
    vol_ref,
    out_ref,
    shear_ref,
    foot_ref,
    slab,
    above,
    below,
    weights,
    fields_even,
    fields_odd,
    sent,
    got,
    staged,
    merged,
    load_sem,
    table_sem,
    row_send,
    row_recv,
    halo_send,
    halo_recv,
    x_send,
    x_recv,
    z_send,
    z_recv,
    known,
):
    slices, rows, columns = vol_ref.shape
    bricks = groups * members
    total = slices * bricks
    tiles = lax.axis_size("tile")
    me, tile = lax.axis_index("depth"), lax.axis_index("tile")
    z, x = me // members, me % members
    span = members * LANES
    wide = members // 2
    tall = rows + 2 * HALO
    decay = -(2.0 / total) * math.log2(math.e)

    half = groups // 2

    code = 0
    for plane, order in enumerate(ORDERS):
        here = 1 - ((z - plane) * (z - plane) + groups * groups - 1) // (groups * groups)
        code = code + here * sum(o * 8**k for k, o in enumerate(order))

    def owner(k):
        power = (1 + 7 * (k % 2)) * (1 + 63 * (k // 2 % 2)) * (1 + 4095 * (k // 4))
        return code // power % 8

    def upper_first(plane):
        return (half - 2 - plane + groups) // groups

    following, leading = me + 1, me - 1
    lower, upper = (tile + 1) % tiles, (tile + tiles - 1) % tiles

    barrier = pltpu.get_barrier_semaphore()

    def greet(depth_id, tile_id):
        pl.semaphore_signal(
            barrier, inc=1, device_id=(depth_id, tile_id), device_id_type=MESH
        )

    for d in range(1, members):
        greet(z * members + (x + d) % members, tile)
    greet(me, lower)
    greet(me, upper)

    def towards(d, act):
        pl.when(z + d < groups)(lambda: act(z + d, 0))
        pl.when(z - d >= 0)(lambda: act(z - d, 1))

    towards(1, lambda other, way: greet(other * members + x, tile))
    pl.when(me < bricks - 1)(lambda: greet(following, tile))
    pl.when(me > 0)(lambda: greet(leading, tile))

    def some(left, count):
        return (left + count - 1) // count

    partners = members + 1 + some(me, bricks) + some(bricks - 1 - me, bricks)
    partners = partners + some(z, groups) + some(groups - 1 - z, groups)

    def tell(level):
        def act(other, way):
            pl.semaphore_signal(
                known.at[level, way],
                inc=1,
                device_id=(other * members + x, tile),
                device_id_type=MESH,
            )

        towards(2**level, act)

    def hear(level):
        towards(
            2**level, lambda other, way: pl.semaphore_wait(known.at[level, 1 - way], 1)
        )

    load = pltpu.make_async_copy(
        vol_ref,
        slab.at[pl.ds(1, slices), pl.ds(0, rows), pl.ds(LANES, columns)],
        load_sem,
    )
    tables = [
        pltpu.make_async_copy(shear_hbm, shear_ref, table_sem.at[0]),
        pltpu.make_async_copy(foot_hbm, foot_ref, table_sem.at[1]),
    ]
    for table in tables:
        table.start()
    load.start()
    pl.semaphore_wait(barrier, partners)
    tell(0)

    blocks = columns // WIDE

    def block_of(plane, u):
        return u + upper_first(plane) * (blocks - 1 - 2 * u)

    def halo(u, up):
        peer = following if up else leading
        start = pl.multiple_of(block_of(peer // members, u) * WIDE, LANES)
        return pltpu.make_async_remote_copy(
            src_ref=vol_ref.at[slices - 1 if up else 0, :, pl.ds(start, WIDE)],
            dst_ref=slab.at[
                0 if up else slices + 1,
                pl.ds(0, rows),
                pl.ds(pl.multiple_of(start + LANES, LANES), WIDE),
            ],
            send_sem=halo_send.at[0 if up else 1, u],
            recv_sem=halo_recv.at[0 if up else 1, u],
            device_id=(peer, tile),
            device_id_type=MESH,
        )

    def row_halo(u, down):
        at = pl.ds(pl.multiple_of(block_of(z, u) * WIDE, LANES), WIDE)
        edge = pl.ds(rows - HALO if down else 0, HALO)
        return pltpu.make_async_remote_copy(
            src_ref=vol_ref.at[:, edge, at],
            dst_ref=(above if down else below).at[:, :, at],
            send_sem=row_send.at[0 if down else 1, u],
            recv_sem=row_recv.at[0 if down else 1, u],
            device_id=(me, lower if down else upper),
            device_id_type=MESH,
        )

    def start_halo(u, carry):
        pl.when(me < bricks - 1)(lambda: halo(u, True).start())
        pl.when(me > 0)(lambda: halo(u, False).start())
        row_halo(u, True).start()
        row_halo(u, False).start()
        return carry

    lax.fori_loop(0, blocks, start_halo, 0)

    slab[:, :, 0:LANES] = jnp.zeros((slices + 2, tall, LANES), slab.dtype)
    slab[:, :, pl.ds(LANES + columns, LANES)] = jnp.zeros(
        (slices + 2, tall, LANES), slab.dtype
    )

    for table in tables:
        table.wait()
    flip = shear_ref[0] > shear_ref[total - 1]

    def weigh(s, carry):
        shift = shear_ref[me * slices + s]
        lead = lax.broadcasted_iota(jnp.int32, (WIDE, WIDE), 0)
        lead = lead - lax.broadcasted_iota(jnp.int32, (WIDE, WIDE), 1)
        for part, base in ((0, LANES), (1, -LANES)):
            at = lead - (base - shift)
            rows_at = pl.ds(part * WIDE, WIDE)
            weights[s, 0, rows_at] = jnp.where(at == 0, 1.0, 0.0).astype(weights.dtype)
            weights[s, 1, rows_at] = jnp.where(
                at == 1, 1.0, jnp.where(at == -1, -1.0, 0.0)
            ).astype(weights.dtype)
        return carry

    lax.fori_loop(0, slices, weigh, 0)

    load.wait()

    def await_rows(u, carry):
        row_halo(u, True).wait_recv()
        row_halo(u, False).wait_recv()
        start = pl.multiple_of(block_of(z, u) * WIDE, LANES)
        at = pl.ds(start, WIDE)
        low = jnp.where(tile < tiles - 1, below[:, :, at].astype(jnp.float32), 0.0)
        high = jnp.where(tile > 0, above[:, :, at].astype(jnp.float32), 0.0)
        at = pl.ds(pl.multiple_of(start + LANES, LANES), WIDE)
        slab[pl.ds(1, slices), pl.ds(rows, 2 * HALO), at] = jnp.concatenate(
            [low, high], axis=1
        ).astype(slab.dtype)
        return carry

    def await_depth(u, carry):
        start = pl.multiple_of(block_of(z, u) * WIDE + LANES, LANES)
        at = pl.ds(start, WIDE)
        pl.when(me > 0)(lambda: halo(u, True).wait_recv())
        pl.when(me < bricks - 1)(lambda: halo(u, False).wait_recv())

        @pl.when(me == 0)
        def _():
            slab[0, pl.ds(0, rows), at] = jnp.zeros((rows, WIDE), slab.dtype)

        @pl.when(me == bricks - 1)
        def _():
            slab[slices + 1, pl.ds(0, rows), at] = jnp.zeros((rows, WIDE), slab.dtype)

        return carry

    def shift_slice(s, start, fields):
        def block(i, j, height):
            at = pl.multiple_of(start + j * WIDE, LANES)
            return slab[i, pl.ds(0, height), pl.ds(at, 2 * WIDE)]

        cur = [block(s + 1, j, tall) for j in range(wide)]
        nxt = [block(s + 2, j, rows) for j in range(wide)]
        prv = [block(s, j, rows) for j in range(wide)]

        def through(blocks, which):
            return jnp.dot(
                jnp.concatenate(blocks, axis=0),
                weights[s, which],
                preferred_element_type=jnp.float32,
            )

        moved = through(cur + nxt + prv, 0)
        sloped = through([b[:rows] for b in cur], 1)
        for j in range(wide):
            strip = moved[j * tall : (j + 1) * tall]
            at = wide * tall + j * rows
            after = moved[at : at + rows]
            at = wide * (tall + rows) + j * rows
            before = moved[at : at + rows]
            down = pltpu.roll(strip, tall - 1, 0)[:rows]
            up = pltpu.roll(strip, 1, 0)[:rows]
            found = (
                strip[:rows],
                down - up,
                sloped[j * rows : (j + 1) * rows],
                after - before,
            )
            for q, value in enumerate(found):
                for h in range(2):
                    fields[q, s, 2 * j + h] = value[:, h * LANES : (h + 1) * LANES]

    def shade_tile(k, i, fields):
        block, part = i // (rows // TILE), i % (rows // TILE)
        at = pl.ds(pl.multiple_of(part * TILE, TILE), TILE)
        shape = (TILE, LANES)
        left = jnp.ones(shape, jnp.float32)
        base = jnp.zeros(shape, jnp.float32)
        tint = [jnp.zeros(shape, jnp.float32)] * 3
        for step in range(slices):
            s = jnp.where(flip, slices - 1 - step, step)
            v = fields[0, s, block, at]
            dx = fields[1, s, block, at]
            dy = fields[2, s, block, at]
            dz = fields[3, s, block, at]
            facing = jnp.abs(
                (0.35 * 0.48) * dx + (0.35 * 0.6) * dy + (0.35 * 0.64) * dz
            )
            shade = 0.15 + facing * lax.rsqrt(dx * dx + dy * dy + dz * dz + 4.0)
            rest = left * jnp.exp2(decay * (v * v))
            weight = (left - rest) * shade
            left = rest
            base = base + weight
            turns = (
                jnp.tanh(0.6 * v + 0.1),
                jnp.tanh(-0.4 * v),
                jnp.tanh(0.25 * v - 0.15),
            )
            tint = [t + weight * turn for t, turn in zip(tint, turns)]
        first = (owner(k) * members + block) * LANES
        column = first + lax.broadcasted_iota(jnp.int32, shape, 1)
        inside = (column >= foot_ref[0, 0]) & (column < foot_ref[0, 1])
        for c, value in enumerate([base + t for t in tint] + [1.0 - left]):
            sent[k, block, c, at] = jnp.where(inside, value, 0.0).astype(sent.dtype)

    def exchange(k, d):
        peer = (x + d) % members
        return pltpu.make_async_remote_copy(
            src_ref=sent.at[k, peer],
            dst_ref=got.at[k, x],
            send_sem=x_send.at[k, d],
            recv_sem=x_recv.at[k, d],
            device_id=(z * members + peer, tile),
            device_id_type=MESH,
        )

    def hand_over(k):
        return pltpu.make_async_remote_copy(
            src_ref=staged.at[k],
            dst_ref=merged.at[z],
            send_sem=z_send.at[k],
            recv_sem=z_recv.at[z],
            device_id=(owner(k) * members + x, tile),
            device_id_type=MESH,
        )

    def handed(g):
        return pltpu.make_async_remote_copy(
            src_ref=staged.at[0],
            dst_ref=merged.at[g],
            send_sem=z_send.at[0],
            recv_sem=z_recv.at[g],
            device_id=(g * members + x, tile),
            device_id_type=MESH,
        )

    def spread(value):
        return jnp.exp2(SPREAD * (value - 0.5))

    def gather(code):
        return jnp.log2(code) * (1.0 / SPREAD) + 0.5

    def merge(k):
        for d in range(1, members):
            exchange(k, d).wait_recv()
        got[k, x] = sent[k, x]

        def part(i, carry):
            at = pl.ds(pl.multiple_of(i * TILE, TILE), TILE)
            pieces = [
                [got[k, b, c, at].astype(jnp.float32) for c in range(4)]
                for b in range(members)
            ]
            for step in range(members):
                piece = [
                    jnp.where(flip, pieces[members - 1 - step][c], pieces[step][c])
                    for c in range(4)
                ]
                if step == 0:
                    colour, left = piece[:3], 1.0 - piece[3]
                else:
                    colour = [p + left * q for p, q in zip(colour, piece[:3])]
                    left = left * (1.0 - piece[3])
            for c, value in enumerate(colour + [left]):
                staged[k, c, at] = spread(value).astype(staged.dtype)
            return carry

        lax.fori_loop(0, rows // TILE, part, 0)

        @pl.when(owner(k) != z)
        def _():
            hand_over(k).start()

        @pl.when(owner(k) == z)
        def _():
            merged[z] = staged[k]

    each = members * (rows // TILE) // slices

    def shade_only(k, fields):
        def body(i, carry):
            for t in range(each):
                shade_tile(k, i * each + t, fields)
            return carry

        lax.fori_loop(0, slices, body, 0)

    def shade_and_shift(k, fields, ahead):
        start = owner(k + 1) * span

        def body(i, carry):
            shift_slice(i, start, ahead)
            for t in range(each):
                shade_tile(k, i * each + t, fields)
            return carry

        lax.fori_loop(0, slices, body, 0, unroll=UNROLL)

    def pass_on(k):
        for d in range(1, members):
            exchange(k, d).start()

        pl.when(k == LAG)(lambda: hear(2))

        @pl.when(k >= LAG)
        def _():
            merge(k - LAG)

    hear(0)
    tell(1)
    soon = half * span // WIDE + 1
    lax.fori_loop(0, soon, await_rows, 0)
    first = owner(0) * span

    def inner(s, carry):
        shift_slice(s, first, fields_even)
        return carry

    lax.fori_loop(1, slices - 1, inner, 0, unroll=(slices - 2) // 2)
    lax.fori_loop(0, soon, await_depth, 0)
    hear(1)
    tell(2)
    shift_slice(0, first, fields_even)
    shift_slice(slices - 1, first, fields_even)

    def advance(h, carry):
        for part, fields, ahead in (
            (0, fields_even, fields_odd),
            (1, fields_odd, fields_even),
        ):
            k = 2 * h + part

            @pl.when(k == half - 2)
            def _():
                lax.fori_loop(soon, blocks, await_rows, 0)
                lax.fori_loop(soon, blocks, await_depth, 0)

            shade_and_shift(k, fields, ahead)
            pass_on(k)
        return carry

    lax.fori_loop(0, groups // 2 - 1, advance, 0)
    shade_and_shift(groups - 2, fields_even, fields_odd)
    pass_on(groups - 2)
    shade_only(groups - 1, fields_odd)
    pass_on(groups - 1)
    def settle(u, carry):
        pl.when(me < bricks - 1)(lambda: halo(u, True).wait_send())
        pl.when(me > 0)(lambda: halo(u, False).wait_send())
        row_halo(u, True).wait_send()
        row_halo(u, False).wait_send()
        return carry

    def sent_on(k, carry):
        for d in range(1, members):
            exchange(k, d).wait_send()

        @pl.when(owner(k) != z)
        def _():
            hand_over(k).wait_send()

        return carry

    lax.fori_loop(0, blocks, settle, 0)
    lax.fori_loop(0, groups - LAG - 1, sent_on, 0)
    for k in range(groups - LAG, groups):
        merge(k)

    def arrive(d, carry):
        handed((z + d) % groups).wait_recv()
        return carry

    lax.fori_loop(1, groups, arrive, 0)

    def finish(i, carry):
        at = pl.ds(pl.multiple_of(i * TILE, TILE), TILE)
        for step in range(groups):
            g = jnp.where(flip, groups - 1 - step, step)
            piece = [gather(merged[g, c, at].astype(jnp.float32)) for c in range(4)]
            if step == 0:
                colour, left = piece[:3], piece[3]
            else:
                colour = [p + left * q for p, q in zip(colour, piece[:3])]
                left = left * piece[3]
        for c, value in enumerate(colour + [1.0 - left]):
            out_ref[c, at] = value
        return carry

    lax.fori_loop(0, rows // TILE, finish, 0)

    lax.fori_loop(groups - LAG - 1, groups, sent_on, 0)


def solution(mesh):
    members = 4
    groups = mesh.shape["depth"] // members

    def shards(volume, shear, footprint):
        slices, rows, columns = volume.shape
        tall = rows + 2 * HALO
        dma = pltpu.SemaphoreType.DMA
        return pl.pallas_call(
            functools.partial(kernel, groups, members),
            out_shape=jax.ShapeDtypeStruct((4, rows, LANES), jnp.float32),
            in_specs=[
                pl.BlockSpec(memory_space=pltpu.HBM),
                pl.BlockSpec(memory_space=pltpu.HBM),
                pl.BlockSpec(memory_space=pltpu.HBM),
            ],
            out_specs=pl.BlockSpec(memory_space=pltpu.VMEM),
            scratch_shapes=[
                pltpu.SMEM(shear.shape, jnp.int32),
                pltpu.SMEM(footprint.shape, jnp.int32),
                pltpu.VMEM((slices + 2, tall, columns + 2 * LANES), jnp.bfloat16),
                pltpu.VMEM((slices, HALO, columns), jnp.bfloat16),
                pltpu.VMEM((slices, HALO, columns), jnp.bfloat16),
                pltpu.VMEM((slices, 2, 2 * WIDE, WIDE), jnp.bfloat16),
                pltpu.VMEM((4, slices, members, rows, LANES), jnp.float32),
                pltpu.VMEM((4, slices, members, rows, LANES), jnp.float32),
                pltpu.VMEM((groups, members, 4, rows, LANES), jnp.bfloat16),
                pltpu.VMEM((groups, members, 4, rows, LANES), jnp.bfloat16),
                pltpu.VMEM((groups, 4, rows, LANES), jnp.bfloat16),
                pltpu.VMEM((groups, 4, rows, LANES), jnp.bfloat16),
                dma,
                dma((2,)),
                dma((2, columns // WIDE)),
                dma((2, columns // WIDE)),
                dma((2, columns // WIDE)),
                dma((2, columns // WIDE)),
                dma((groups, members)),
                dma((groups, members)),
                dma((groups,)),
                dma((groups,)),
                pltpu.SemaphoreType.REGULAR((3, 2)),
            ],
            compiler_params=pltpu.CompilerParams(
                collective_id=0,
                has_side_effects=True,
                vmem_limit_bytes=48 * 2**20,
            ),
        )(*(pltpu.with_memory_space_constraint(a, pltpu.HBM) for a in (shear, footprint, volume)))

    return jax.shard_map(
        shards,
        mesh=mesh,
        in_specs=(P("depth", "tile", None), P(), P("depth", None)),
        out_specs=P(None, "tile", "depth"),
        check_vma=False,
    )
```

```python
import functools
import math

import jax
import jax.numpy as jnp
from jax import lax
from jax.experimental import pallas as pl
from jax.experimental.pallas import tpu as pltpu
from jax.sharding import PartitionSpec as P

MESH = pl.DeviceIdType.MESH
LANES = 128
WIDE = 2 * LANES
HALO = 8
LAG = 3
TILE = 16
UNROLL = 2
SPREAD = 200.0
ORDERS = (
    (4, 5, 6, 7, 1, 2, 3, 0),
    (5, 6, 7, 4, 0, 2, 3, 1),
    (6, 7, 4, 5, 0, 1, 3, 2),
    (0, 1, 2, 7, 6, 5, 4, 3),
    (0, 1, 2, 3, 7, 6, 5, 4),
    (1, 2, 3, 0, 7, 4, 6, 5),
    (2, 3, 0, 1, 4, 7, 5, 6),
    (3, 0, 1, 2, 4, 5, 6, 7),
)


def kernel(
    groups,
    members,
    shear_hbm,
    foot_hbm,
    vol_ref,
    out_ref,
    shear_ref,
    foot_ref,
    slab,
    above,
    below,
    weights,
    fields_even,
    fields_odd,
    sent,
    got,
    staged,
    merged,
    load_sem,
    table_sem,
    row_send,
    row_recv,
    halo_send,
    halo_recv,
    x_send,
    x_recv,
    z_send,
    z_recv,
    known,
):
    slices, rows, columns = vol_ref.shape
    bricks = groups * members
    total = slices * bricks
    tiles = lax.axis_size("tile")
    me, tile = lax.axis_index("depth"), lax.axis_index("tile")
    z, x = me // members, me % members
    span = members * LANES
    wide = members // 2
    tall = rows + 2 * HALO
    decay = -(2.0 / total) * math.log2(math.e)

    half = groups // 2

    code = 0
    for plane, order in enumerate(ORDERS):
        here = 1 - ((z - plane) * (z - plane) + groups * groups - 1) // (groups * groups)
        code = code + here * sum(o * 8**k for k, o in enumerate(order))

    def owner(k):
        power = (1 + 7 * (k % 2)) * (1 + 63 * (k // 2 % 2)) * (1 + 4095 * (k // 4))
        return code // power % 8

    def upper_first(plane):
        return (half - 2 - plane + groups) // groups

    following, leading = me + 1, me - 1
    lower, upper = (tile + 1) % tiles, (tile + tiles - 1) % tiles

    barrier = pltpu.get_barrier_semaphore()

    def greet(depth_id, tile_id):
        pl.semaphore_signal(
            barrier, inc=1, device_id=(depth_id, tile_id), device_id_type=MESH
        )

    for d in range(1, members):
        greet(z * members + (x + d) % members, tile)
    greet(me, lower)
    greet(me, upper)

    def towards(d, act):
        pl.when(z + d < groups)(lambda: act(z + d, 0))
        pl.when(z - d >= 0)(lambda: act(z - d, 1))

    towards(1, lambda other, way: greet(other * members + x, tile))
    pl.when(me < bricks - 1)(lambda: greet(following, tile))
    pl.when(me > 0)(lambda: greet(leading, tile))

    def some(left, count):
        return (left + count - 1) // count

    partners = members + 1 + some(me, bricks) + some(bricks - 1 - me, bricks)
    partners = partners + some(z, groups) + some(groups - 1 - z, groups)

    def tell(level):
        def act(other, way):
            pl.semaphore_signal(
                known.at[level, way],
                inc=1,
                device_id=(other * members + x, tile),
                device_id_type=MESH,
            )

        towards(2**level, act)

    def hear(level):
        towards(
            2**level, lambda other, way: pl.semaphore_wait(known.at[level, 1 - way], 1)
        )

    load = pltpu.make_async_copy(
        vol_ref,
        slab.at[pl.ds(1, slices), pl.ds(0, rows), pl.ds(LANES, columns)],
        load_sem,
    )
    tables = [
        pltpu.make_async_copy(shear_hbm, shear_ref, table_sem.at[0]),
        pltpu.make_async_copy(foot_hbm, foot_ref, table_sem.at[1]),
    ]
    for table in tables:
        table.start()
    load.start()
    pl.semaphore_wait(barrier, partners)
    tell(0)

    blocks = columns // WIDE

    def block_of(plane, u):
        return u + upper_first(plane) * (blocks - 1 - 2 * u)

    def halo(u, up):
        peer = following if up else leading
        start = pl.multiple_of(block_of(peer // members, u) * WIDE, LANES)
        return pltpu.make_async_remote_copy(
            src_ref=vol_ref.at[slices - 1 if up else 0, :, pl.ds(start, WIDE)],
            dst_ref=slab.at[
                0 if up else slices + 1,
                pl.ds(0, rows),
                pl.ds(pl.multiple_of(start + LANES, LANES), WIDE),
            ],
            send_sem=halo_send.at[0 if up else 1, u],
            recv_sem=halo_recv.at[0 if up else 1, u],
            device_id=(peer, tile),
            device_id_type=MESH,
        )

    def row_halo(u, down):
        at = pl.ds(pl.multiple_of(block_of(z, u) * WIDE, LANES), WIDE)
        edge = pl.ds(rows - HALO if down else 0, HALO)
        return pltpu.make_async_remote_copy(
            src_ref=vol_ref.at[:, edge, at],
            dst_ref=(above if down else below).at[:, :, at],
            send_sem=row_send.at[0 if down else 1, u],
            recv_sem=row_recv.at[0 if down else 1, u],
            device_id=(me, lower if down else upper),
            device_id_type=MESH,
        )

    def start_halo(u, carry):
        pl.when(me < bricks - 1)(lambda: halo(u, True).start())
        pl.when(me > 0)(lambda: halo(u, False).start())
        row_halo(u, True).start()
        row_halo(u, False).start()
        return carry

    lax.fori_loop(0, blocks, start_halo, 0)

    slab[:, :, 0:LANES] = jnp.zeros((slices + 2, tall, LANES), slab.dtype)
    slab[:, :, pl.ds(LANES + columns, LANES)] = jnp.zeros(
        (slices + 2, tall, LANES), slab.dtype
    )

    for table in tables:
        table.wait()
    flip = shear_ref[0] > shear_ref[total - 1]

    def weigh(s, carry):
        shift = shear_ref[me * slices + s]
        lead = lax.broadcasted_iota(jnp.int32, (WIDE, WIDE), 0)
        lead = lead - lax.broadcasted_iota(jnp.int32, (WIDE, WIDE), 1)
        for part, base in ((0, LANES), (1, -LANES)):
            at = lead - (base - shift)
            rows_at = pl.ds(part * WIDE, WIDE)
            weights[s, 0, rows_at] = jnp.where(at == 0, 1.0, 0.0).astype(weights.dtype)
            weights[s, 1, rows_at] = jnp.where(
                at == 1, 1.0, jnp.where(at == -1, -1.0, 0.0)
            ).astype(weights.dtype)
        return carry

    lax.fori_loop(0, slices, weigh, 0)

    load.wait()

    def await_rows(u, carry):
        row_halo(u, True).wait_recv()
        row_halo(u, False).wait_recv()
        start = pl.multiple_of(block_of(z, u) * WIDE, LANES)
        at = pl.ds(start, WIDE)
        low = jnp.where(tile < tiles - 1, below[:, :, at].astype(jnp.float32), 0.0)
        high = jnp.where(tile > 0, above[:, :, at].astype(jnp.float32), 0.0)
        at = pl.ds(pl.multiple_of(start + LANES, LANES), WIDE)
        slab[pl.ds(1, slices), pl.ds(rows, 2 * HALO), at] = jnp.concatenate(
            [low, high], axis=1
        ).astype(slab.dtype)
        return carry

    def await_depth(u, carry):
        start = pl.multiple_of(block_of(z, u) * WIDE + LANES, LANES)
        at = pl.ds(start, WIDE)
        pl.when(me > 0)(lambda: halo(u, True).wait_recv())
        pl.when(me < bricks - 1)(lambda: halo(u, False).wait_recv())

        @pl.when(me == 0)
        def _():
            slab[0, pl.ds(0, rows), at] = jnp.zeros((rows, WIDE), slab.dtype)

        @pl.when(me == bricks - 1)
        def _():
            slab[slices + 1, pl.ds(0, rows), at] = jnp.zeros((rows, WIDE), slab.dtype)

        return carry

    def shift_slice(s, start, fields):
        def block(i, j, height):
            at = pl.multiple_of(start + j * WIDE, LANES)
            return slab[i, pl.ds(0, height), pl.ds(at, 2 * WIDE)]

        cur = [block(s + 1, j, tall) for j in range(wide)]
        nxt = [block(s + 2, j, rows) for j in range(wide)]
        prv = [block(s, j, rows) for j in range(wide)]

        def through(blocks, which):
            return jnp.dot(
                jnp.concatenate(blocks, axis=0),
                weights[s, which],
                preferred_element_type=jnp.float32,
            )

        moved = through(cur + nxt + prv, 0)
        sloped = through([b[:rows] for b in cur], 1)
        for j in range(wide):
            strip = moved[j * tall : (j + 1) * tall]
            at = wide * tall + j * rows
            after = moved[at : at + rows]
            at = wide * (tall + rows) + j * rows
            before = moved[at : at + rows]
            down = pltpu.roll(strip, tall - 1, 0)[:rows]
            up = pltpu.roll(strip, 1, 0)[:rows]
            found = (
                strip[:rows],
                down - up,
                sloped[j * rows : (j + 1) * rows],
                after - before,
            )
            for q, value in enumerate(found):
                for h in range(2):
                    fields[q, s, 2 * j + h] = value[:, h * LANES : (h + 1) * LANES]

    def shade_tile(k, i, fields):
        block, part = i // (rows // TILE), i % (rows // TILE)
        at = pl.ds(pl.multiple_of(part * TILE, TILE), TILE)
        shape = (TILE, LANES)
        left = jnp.ones(shape, jnp.float32)
        base = jnp.zeros(shape, jnp.float32)
        tint = [jnp.zeros(shape, jnp.float32)] * 3
        for step in range(slices):
            s = jnp.where(flip, slices - 1 - step, step)
            v = fields[0, s, block, at]
            dx = fields[1, s, block, at]
            dy = fields[2, s, block, at]
            dz = fields[3, s, block, at]
            facing = jnp.abs(
                (0.35 * 0.48) * dx + (0.35 * 0.6) * dy + (0.35 * 0.64) * dz
            )
            shade = 0.15 + facing * lax.rsqrt(dx * dx + dy * dy + dz * dz + 4.0)
            rest = left * jnp.exp2(decay * (v * v))
            weight = (left - rest) * shade
            left = rest
            base = base + weight
            turns = (
                jnp.tanh(0.6 * v + 0.1),
                jnp.tanh(-0.4 * v),
                jnp.tanh(0.25 * v - 0.15),
            )
            tint = [t + weight * turn for t, turn in zip(tint, turns)]
        first = (owner(k) * members + block) * LANES
        column = first + lax.broadcasted_iota(jnp.int32, shape, 1)
        inside = (column >= foot_ref[0, 0]) & (column < foot_ref[0, 1])
        for c, value in enumerate([base + t for t in tint] + [1.0 - left]):
            sent[k, block, c, at] = jnp.where(inside, value, 0.0).astype(sent.dtype)

    def exchange(k, d):
        peer = (x + d) % members
        return pltpu.make_async_remote_copy(
            src_ref=sent.at[k, peer],
            dst_ref=got.at[k, x],
            send_sem=x_send.at[k, d],
            recv_sem=x_recv.at[k, d],
            device_id=(z * members + peer, tile),
            device_id_type=MESH,
        )

    def hand_over(k):
        return pltpu.make_async_remote_copy(
            src_ref=staged.at[k],
            dst_ref=merged.at[z],
            send_sem=z_send.at[k],
            recv_sem=z_recv.at[z],
            device_id=(owner(k) * members + x, tile),
            device_id_type=MESH,
        )

    def handed(g):
        return pltpu.make_async_remote_copy(
            src_ref=staged.at[0],
            dst_ref=merged.at[g],
            send_sem=z_send.at[0],
            recv_sem=z_recv.at[g],
            device_id=(g * members + x, tile),
            device_id_type=MESH,
        )

    def spread(value):
        return jnp.exp2(SPREAD * (value - 0.5))

    def gather(code):
        return jnp.log2(code) * (1.0 / SPREAD) + 0.5

    def merge(k):
        for d in range(1, members):
            exchange(k, d).wait_recv()
        got[k, x] = sent[k, x]

        def part(i, carry):
            at = pl.ds(pl.multiple_of(i * TILE, TILE), TILE)
            pieces = [
                [got[k, b, c, at].astype(jnp.float32) for c in range(4)]
                for b in range(members)
            ]
            for step in range(members):
                piece = [
                    jnp.where(flip, pieces[members - 1 - step][c], pieces[step][c])
                    for c in range(4)
                ]
                if step == 0:
                    colour, left = piece[:3], 1.0 - piece[3]
                else:
                    colour = [p + left * q for p, q in zip(colour, piece[:3])]
                    left = left * (1.0 - piece[3])
            for c, value in enumerate(colour + [left]):
                staged[k, c, at] = spread(value).astype(staged.dtype)
            return carry

        lax.fori_loop(0, rows // TILE, part, 0)

        @pl.when(owner(k) != z)
        def _():
            hand_over(k).start()

        @pl.when(owner(k) == z)
        def _():
            merged[z] = staged[k]

    each = members * (rows // TILE) // slices

    def shade_only(k, fields):
        def body(i, carry):
            for t in range(each):
                shade_tile(k, i * each + t, fields)
            return carry

        lax.fori_loop(0, slices, body, 0)

    def shade_and_shift(k, fields, ahead):
        start = owner(k + 1) * span

        def body(i, carry):
            shift_slice(i, start, ahead)
            for t in range(each):
                shade_tile(k, i * each + t, fields)
            return carry

        lax.fori_loop(0, slices, body, 0, unroll=UNROLL)

    def pass_on(k):
        for d in (members // 2, 1, members - 1):
            exchange(k, d).start()

        pl.when(k == LAG)(lambda: hear(2))

        @pl.when(k >= LAG)
        def _():
            merge(k - LAG)

    hear(0)
    tell(1)
    soon = half * span // WIDE + 1
    lax.fori_loop(0, soon, await_rows, 0)
    first = owner(0) * span

    def inner(s, carry):
        shift_slice(s, first, fields_even)
        return carry

    lax.fori_loop(1, slices - 1, inner, 0, unroll=(slices - 2) // 2)
    lax.fori_loop(0, soon, await_depth, 0)
    hear(1)
    tell(2)
    shift_slice(0, first, fields_even)
    shift_slice(slices - 1, first, fields_even)

    def advance(h, carry):
        for part, fields, ahead in (
            (0, fields_even, fields_odd),
            (1, fields_odd, fields_even),
        ):
            k = 2 * h + part

            @pl.when(k == half - 2)
            def _():
                lax.fori_loop(soon, blocks, await_rows, 0)
                lax.fori_loop(soon, blocks, await_depth, 0)

            shade_and_shift(k, fields, ahead)
            pass_on(k)
        return carry

    lax.fori_loop(0, groups // 2 - 1, advance, 0)
    shade_and_shift(groups - 2, fields_even, fields_odd)
    pass_on(groups - 2)
    shade_only(groups - 1, fields_odd)
    pass_on(groups - 1)
    def settle(u, carry):
        pl.when(me < bricks - 1)(lambda: halo(u, True).wait_send())
        pl.when(me > 0)(lambda: halo(u, False).wait_send())
        row_halo(u, True).wait_send()
        row_halo(u, False).wait_send()
        return carry

    def sent_on(k, carry):
        for d in range(1, members):
            exchange(k, d).wait_send()

        @pl.when(owner(k) != z)
        def _():
            hand_over(k).wait_send()

        return carry

    lax.fori_loop(0, blocks, settle, 0)
    lax.fori_loop(0, groups - LAG - 1, sent_on, 0)
    for k in range(groups - LAG, groups):
        merge(k)

    def arrive(d, carry):
        handed((z + d) % groups).wait_recv()
        return carry

    lax.fori_loop(1, groups, arrive, 0)

    def finish(i, carry):
        at = pl.ds(pl.multiple_of(i * TILE, TILE), TILE)
        for step in range(groups):
            g = jnp.where(flip, groups - 1 - step, step)
            piece = [gather(merged[g, c, at].astype(jnp.float32)) for c in range(4)]
            if step == 0:
                colour, left = piece[:3], piece[3]
            else:
                colour = [p + left * q for p, q in zip(colour, piece[:3])]
                left = left * piece[3]
        for c, value in enumerate(colour + [1.0 - left]):
            out_ref[c, at] = value
        return carry

    lax.fori_loop(0, rows // TILE, finish, 0)

    lax.fori_loop(groups - LAG - 1, groups, sent_on, 0)


def solution(mesh):
    members = 4
    groups = mesh.shape["depth"] // members

    def shards(volume, shear, footprint):
        slices, rows, columns = volume.shape
        tall = rows + 2 * HALO
        dma = pltpu.SemaphoreType.DMA
        return pl.pallas_call(
            functools.partial(kernel, groups, members),
            out_shape=jax.ShapeDtypeStruct((4, rows, LANES), jnp.float32),
            in_specs=[
                pl.BlockSpec(memory_space=pltpu.HBM),
                pl.BlockSpec(memory_space=pltpu.HBM),
                pl.BlockSpec(memory_space=pltpu.HBM),
            ],
            out_specs=pl.BlockSpec(memory_space=pltpu.VMEM),
            scratch_shapes=[
                pltpu.SMEM(shear.shape, jnp.int32),
                pltpu.SMEM(footprint.shape, jnp.int32),
                pltpu.VMEM((slices + 2, tall, columns + 2 * LANES), jnp.bfloat16),
                pltpu.VMEM((slices, HALO, columns), jnp.bfloat16),
                pltpu.VMEM((slices, HALO, columns), jnp.bfloat16),
                pltpu.VMEM((slices, 2, 2 * WIDE, WIDE), jnp.bfloat16),
                pltpu.VMEM((4, slices, members, rows, LANES), jnp.float32),
                pltpu.VMEM((4, slices, members, rows, LANES), jnp.float32),
                pltpu.VMEM((groups, members, 4, rows, LANES), jnp.bfloat16),
                pltpu.VMEM((groups, members, 4, rows, LANES), jnp.bfloat16),
                pltpu.VMEM((groups, 4, rows, LANES), jnp.bfloat16),
                pltpu.VMEM((groups, 4, rows, LANES), jnp.bfloat16),
                dma,
                dma((2,)),
                dma((2, columns // WIDE)),
                dma((2, columns // WIDE)),
                dma((2, columns // WIDE)),
                dma((2, columns // WIDE)),
                dma((groups, members)),
                dma((groups, members)),
                dma((groups,)),
                dma((groups,)),
                pltpu.SemaphoreType.REGULAR((3, 2)),
            ],
            compiler_params=pltpu.CompilerParams(
                collective_id=0,
                has_side_effects=True,
                vmem_limit_bytes=48 * 2**20,
            ),
        )(*(pltpu.with_memory_space_constraint(a, pltpu.HBM) for a in (shear, footprint, volume)))

    return jax.shard_map(
        shards,
        mesh=mesh,
        in_specs=(P("depth", "tile", None), P(), P("depth", None)),
        out_specs=P(None, "tile", "depth"),
        check_vma=False,
    )
```

```python
import functools
import math

import jax
import jax.numpy as jnp
from jax import lax
from jax.experimental import pallas as pl
from jax.experimental.pallas import tpu as pltpu
from jax.sharding import PartitionSpec as P

MESH = pl.DeviceIdType.MESH
LANES = 128
WIDE = 2 * LANES
HALO = 8
LAG = 3
TILE = 16
UNROLL = 2
SPREAD = 200.0
ORDERS = (
    (4, 5, 6, 7, 1, 2, 3, 0),
    (5, 6, 7, 4, 0, 2, 3, 1),
    (6, 7, 4, 5, 0, 1, 3, 2),
    (0, 1, 2, 7, 6, 5, 4, 3),
    (0, 1, 2, 3, 7, 6, 5, 4),
    (1, 2, 3, 0, 7, 4, 6, 5),
    (2, 3, 0, 1, 4, 7, 5, 6),
    (3, 0, 1, 2, 4, 5, 6, 7),
)


def kernel(
    groups,
    members,
    shear_hbm,
    foot_hbm,
    vol_ref,
    out_ref,
    shear_ref,
    foot_ref,
    slab,
    above,
    below,
    weights,
    fields_even,
    fields_odd,
    sent,
    got,
    staged,
    merged,
    load_sem,
    table_sem,
    row_send,
    row_recv,
    halo_send,
    halo_recv,
    x_send,
    x_recv,
    z_send,
    z_recv,
    known,
):
    slices, rows, columns = vol_ref.shape
    bricks = groups * members
    total = slices * bricks
    tiles = lax.axis_size("tile")
    me, tile = lax.axis_index("depth"), lax.axis_index("tile")
    z, x = me // members, me % members
    span = members * LANES
    wide = members // 2
    tall = rows + 2 * HALO
    decay = -(2.0 / total) * math.log2(math.e)

    half = groups // 2

    code = 0
    for plane, order in enumerate(ORDERS):
        here = 1 - ((z - plane) * (z - plane) + groups * groups - 1) // (groups * groups)
        code = code + here * sum(o * 8**k for k, o in enumerate(order))

    def owner(k):
        power = (1 + 7 * (k % 2)) * (1 + 63 * (k // 2 % 2)) * (1 + 4095 * (k // 4))
        return code // power % 8

    def upper_first(plane):
        return (half - 2 - plane + groups) // groups

    following, leading = me + 1, me - 1
    lower, upper = (tile + 1) % tiles, (tile + tiles - 1) % tiles

    barrier = pltpu.get_barrier_semaphore()

    def greet(depth_id, tile_id):
        pl.semaphore_signal(
            barrier, inc=1, device_id=(depth_id, tile_id), device_id_type=MESH
        )

    for d in range(1, members):
        greet(z * members + (x + d) % members, tile)
    greet(me, lower)
    greet(me, upper)

    def towards(d, act):
        pl.when(z + d < groups)(lambda: act(z + d, 0))
        pl.when(z - d >= 0)(lambda: act(z - d, 1))

    towards(1, lambda other, way: greet(other * members + x, tile))
    pl.when(me < bricks - 1)(lambda: greet(following, tile))
    pl.when(me > 0)(lambda: greet(leading, tile))

    def some(left, count):
        return (left + count - 1) // count

    partners = members + 1 + some(me, bricks) + some(bricks - 1 - me, bricks)
    partners = partners + some(z, groups) + some(groups - 1 - z, groups)

    def tell(level):
        def act(other, way):
            pl.semaphore_signal(
                known.at[level, way],
                inc=1,
                device_id=(other * members + x, tile),
                device_id_type=MESH,
            )

        towards(2**level, act)

    def hear(level):
        towards(
            2**level, lambda other, way: pl.semaphore_wait(known.at[level, 1 - way], 1)
        )

    load = pltpu.make_async_copy(
        vol_ref,
        slab.at[pl.ds(1, slices), pl.ds(0, rows), pl.ds(LANES, columns)],
        load_sem,
    )
    tables = [
        pltpu.make_async_copy(shear_hbm, shear_ref, table_sem.at[0]),
        pltpu.make_async_copy(foot_hbm, foot_ref, table_sem.at[1]),
    ]
    for table in tables:
        table.start()
    load.start()
    pl.semaphore_wait(barrier, partners)
    tell(0)

    blocks = columns // WIDE

    def block_of(plane, u):
        return u + upper_first(plane) * (blocks - 1 - 2 * u)

    def halo(u, up):
        peer = following if up else leading
        start = pl.multiple_of(block_of(peer // members, u) * WIDE, LANES)
        return pltpu.make_async_remote_copy(
            src_ref=vol_ref.at[slices - 1 if up else 0, :, pl.ds(start, WIDE)],
            dst_ref=slab.at[
                0 if up else slices + 1,
                pl.ds(0, rows),
                pl.ds(pl.multiple_of(start + LANES, LANES), WIDE),
            ],
            send_sem=halo_send.at[0 if up else 1, u],
            recv_sem=halo_recv.at[0 if up else 1, u],
            device_id=(peer, tile),
            device_id_type=MESH,
        )

    def row_halo(u, down):
        at = pl.ds(pl.multiple_of(block_of(z, u) * WIDE, LANES), WIDE)
        edge = pl.ds(rows - HALO if down else 0, HALO)
        return pltpu.make_async_remote_copy(
            src_ref=vol_ref.at[:, edge, at],
            dst_ref=(above if down else below).at[:, :, at],
            send_sem=row_send.at[0 if down else 1, u],
            recv_sem=row_recv.at[0 if down else 1, u],
            device_id=(me, lower if down else upper),
            device_id_type=MESH,
        )

    def start_halo(u, carry):
        pl.when((me > 0) & (x == 0))(lambda: halo(u, False).start())
        pl.when(me < bricks - 1)(lambda: halo(u, True).start())
        pl.when((me > 0) & (x > 0))(lambda: halo(u, False).start())
        row_halo(u, True).start()
        row_halo(u, False).start()
        return carry

    lax.fori_loop(0, blocks, start_halo, 0)

    slab[:, :, 0:LANES] = jnp.zeros((slices + 2, tall, LANES), slab.dtype)
    slab[:, :, pl.ds(LANES + columns, LANES)] = jnp.zeros(
        (slices + 2, tall, LANES), slab.dtype
    )

    for table in tables:
        table.wait()
    flip = shear_ref[0] > shear_ref[total - 1]

    def weigh(s, carry):
        shift = shear_ref[me * slices + s]
        lead = lax.broadcasted_iota(jnp.int32, (WIDE, WIDE), 0)
        lead = lead - lax.broadcasted_iota(jnp.int32, (WIDE, WIDE), 1)
        for part, base in ((0, LANES), (1, -LANES)):
            at = lead - (base - shift)
            rows_at = pl.ds(part * WIDE, WIDE)
            weights[s, 0, rows_at] = jnp.where(at == 0, 1.0, 0.0).astype(weights.dtype)
            weights[s, 1, rows_at] = jnp.where(
                at == 1, 1.0, jnp.where(at == -1, -1.0, 0.0)
            ).astype(weights.dtype)
        return carry

    lax.fori_loop(0, slices, weigh, 0)

    load.wait()

    def await_rows(u, carry):
        row_halo(u, True).wait_recv()
        row_halo(u, False).wait_recv()
        start = pl.multiple_of(block_of(z, u) * WIDE, LANES)
        at = pl.ds(start, WIDE)
        low = jnp.where(tile < tiles - 1, below[:, :, at].astype(jnp.float32), 0.0)
        high = jnp.where(tile > 0, above[:, :, at].astype(jnp.float32), 0.0)
        at = pl.ds(pl.multiple_of(start + LANES, LANES), WIDE)
        slab[pl.ds(1, slices), pl.ds(rows, 2 * HALO), at] = jnp.concatenate(
            [low, high], axis=1
        ).astype(slab.dtype)
        return carry

    def await_depth(u, carry):
        start = pl.multiple_of(block_of(z, u) * WIDE + LANES, LANES)
        at = pl.ds(start, WIDE)
        pl.when(me > 0)(lambda: halo(u, True).wait_recv())
        pl.when(me < bricks - 1)(lambda: halo(u, False).wait_recv())

        @pl.when(me == 0)
        def _():
            slab[0, pl.ds(0, rows), at] = jnp.zeros((rows, WIDE), slab.dtype)

        @pl.when(me == bricks - 1)
        def _():
            slab[slices + 1, pl.ds(0, rows), at] = jnp.zeros((rows, WIDE), slab.dtype)

        return carry

    def shift_slice(s, start, fields):
        def block(i, j, height):
            at = pl.multiple_of(start + j * WIDE, LANES)
            return slab[i, pl.ds(0, height), pl.ds(at, 2 * WIDE)]

        cur = [block(s + 1, j, tall) for j in range(wide)]
        nxt = [block(s + 2, j, rows) for j in range(wide)]
        prv = [block(s, j, rows) for j in range(wide)]

        def through(blocks, which):
            return jnp.dot(
                jnp.concatenate(blocks, axis=0),
                weights[s, which],
                preferred_element_type=jnp.float32,
            )

        moved = through(cur + nxt + prv, 0)
        sloped = through([b[:rows] for b in cur], 1)
        for j in range(wide):
            strip = moved[j * tall : (j + 1) * tall]
            at = wide * tall + j * rows
            after = moved[at : at + rows]
            at = wide * (tall + rows) + j * rows
            before = moved[at : at + rows]
            down = pltpu.roll(strip, tall - 1, 0)[:rows]
            up = pltpu.roll(strip, 1, 0)[:rows]
            found = (
                strip[:rows],
                down - up,
                sloped[j * rows : (j + 1) * rows],
                after - before,
            )
            for q, value in enumerate(found):
                for h in range(2):
                    fields[q, s, 2 * j + h] = value[:, h * LANES : (h + 1) * LANES]

    def shade_tile(k, i, fields):
        block, part = i // (rows // TILE), i % (rows // TILE)
        at = pl.ds(pl.multiple_of(part * TILE, TILE), TILE)
        shape = (TILE, LANES)
        left = jnp.ones(shape, jnp.float32)
        base = jnp.zeros(shape, jnp.float32)
        tint = [jnp.zeros(shape, jnp.float32)] * 3
        for step in range(slices):
            s = jnp.where(flip, slices - 1 - step, step)
            v = fields[0, s, block, at]
            dx = fields[1, s, block, at]
            dy = fields[2, s, block, at]
            dz = fields[3, s, block, at]
            facing = jnp.abs(
                (0.35 * 0.48) * dx + (0.35 * 0.6) * dy + (0.35 * 0.64) * dz
            )
            shade = 0.15 + facing * lax.rsqrt(dx * dx + dy * dy + dz * dz + 4.0)
            rest = left * jnp.exp2(decay * (v * v))
            weight = (left - rest) * shade
            left = rest
            base = base + weight
            turns = (
                jnp.tanh(0.6 * v + 0.1),
                jnp.tanh(-0.4 * v),
                jnp.tanh(0.25 * v - 0.15),
            )
            tint = [t + weight * turn for t, turn in zip(tint, turns)]
        first = (owner(k) * members + block) * LANES
        column = first + lax.broadcasted_iota(jnp.int32, shape, 1)
        inside = (column >= foot_ref[0, 0]) & (column < foot_ref[0, 1])
        for c, value in enumerate([base + t for t in tint] + [1.0 - left]):
            sent[k, block, c, at] = jnp.where(inside, value, 0.0).astype(sent.dtype)

    def exchange(k, d):
        peer = (x + d) % members
        return pltpu.make_async_remote_copy(
            src_ref=sent.at[k, peer],
            dst_ref=got.at[k, x],
            send_sem=x_send.at[k, d],
            recv_sem=x_recv.at[k, d],
            device_id=(z * members + peer, tile),
            device_id_type=MESH,
        )

    def hand_over(k):
        return pltpu.make_async_remote_copy(
            src_ref=staged.at[k],
            dst_ref=merged.at[z],
            send_sem=z_send.at[k],
            recv_sem=z_recv.at[z],
            device_id=(owner(k) * members + x, tile),
            device_id_type=MESH,
        )

    def handed(g):
        return pltpu.make_async_remote_copy(
            src_ref=staged.at[0],
            dst_ref=merged.at[g],
            send_sem=z_send.at[0],
            recv_sem=z_recv.at[g],
            device_id=(g * members + x, tile),
            device_id_type=MESH,
        )

    def spread(value):
        return jnp.exp2(SPREAD * (value - 0.5))

    def gather(code):
        return jnp.log2(code) * (1.0 / SPREAD) + 0.5

    def merge(k):
        for d in range(1, members):
            exchange(k, d).wait_recv()
        got[k, x] = sent[k, x]

        def part(i, carry):
            at = pl.ds(pl.multiple_of(i * TILE, TILE), TILE)
            pieces = [
                [got[k, b, c, at].astype(jnp.float32) for c in range(4)]
                for b in range(members)
            ]
            for step in range(members):
                piece = [
                    jnp.where(flip, pieces[members - 1 - step][c], pieces[step][c])
                    for c in range(4)
                ]
                if step == 0:
                    colour, left = piece[:3], 1.0 - piece[3]
                else:
                    colour = [p + left * q for p, q in zip(colour, piece[:3])]
                    left = left * (1.0 - piece[3])
            for c, value in enumerate(colour + [left]):
                staged[k, c, at] = spread(value).astype(staged.dtype)
            return carry

        lax.fori_loop(0, rows // TILE, part, 0)

        @pl.when(owner(k) != z)
        def _():
            hand_over(k).start()

        @pl.when(owner(k) == z)
        def _():
            merged[z] = staged[k]

    each = members * (rows // TILE) // slices

    def shade_only(k, fields):
        def body(i, carry):
            for t in range(each):
                shade_tile(k, i * each + t, fields)
            return carry

        lax.fori_loop(0, slices, body, 0)

    def shade_and_shift(k, fields, ahead):
        start = owner(k + 1) * span

        def body(i, carry):
            shift_slice(i, start, ahead)
            for t in range(each):
                shade_tile(k, i * each + t, fields)
            return carry

        lax.fori_loop(0, slices, body, 0, unroll=UNROLL)

    def pass_on(k):
        for d in (members // 2, 1, members - 1):
            exchange(k, d).start()

        pl.when(k == LAG)(lambda: hear(2))

        @pl.when(k >= LAG)
        def _():
            merge(k - LAG)

    hear(0)
    tell(1)
    soon = half * span // WIDE + 1
    lax.fori_loop(0, soon, await_rows, 0)
    first = owner(0) * span

    def inner(s, carry):
        shift_slice(s, first, fields_even)
        return carry

    lax.fori_loop(1, slices - 1, inner, 0, unroll=(slices - 2) // 2)
    lax.fori_loop(0, soon, await_depth, 0)
    hear(1)
    tell(2)
    shift_slice(0, first, fields_even)
    shift_slice(slices - 1, first, fields_even)

    def advance(h, carry):
        for part, fields, ahead in (
            (0, fields_even, fields_odd),
            (1, fields_odd, fields_even),
        ):
            k = 2 * h + part

            @pl.when(k == half - 2)
            def _():
                lax.fori_loop(soon, blocks, await_rows, 0)
                lax.fori_loop(soon, blocks, await_depth, 0)

            shade_and_shift(k, fields, ahead)
            pass_on(k)
        return carry

    lax.fori_loop(0, groups // 2 - 1, advance, 0)
    shade_and_shift(groups - 2, fields_even, fields_odd)
    pass_on(groups - 2)
    shade_only(groups - 1, fields_odd)
    pass_on(groups - 1)
    def settle(u, carry):
        pl.when(me < bricks - 1)(lambda: halo(u, True).wait_send())
        pl.when(me > 0)(lambda: halo(u, False).wait_send())
        row_halo(u, True).wait_send()
        row_halo(u, False).wait_send()
        return carry

    def sent_on(k, carry):
        for d in range(1, members):
            exchange(k, d).wait_send()

        @pl.when(owner(k) != z)
        def _():
            hand_over(k).wait_send()

        return carry

    lax.fori_loop(0, blocks, settle, 0)
    lax.fori_loop(0, groups - LAG - 1, sent_on, 0)
    for k in range(groups - LAG, groups):
        merge(k)

    def arrive(d, carry):
        handed((z + d) % groups).wait_recv()
        return carry

    lax.fori_loop(1, groups, arrive, 0)

    def finish(i, carry):
        at = pl.ds(pl.multiple_of(i * TILE, TILE), TILE)
        for step in range(groups):
            g = jnp.where(flip, groups - 1 - step, step)
            piece = [gather(merged[g, c, at].astype(jnp.float32)) for c in range(4)]
            if step == 0:
                colour, left = piece[:3], piece[3]
            else:
                colour = [p + left * q for p, q in zip(colour, piece[:3])]
                left = left * piece[3]
        for c, value in enumerate(colour + [1.0 - left]):
            out_ref[c, at] = value
        return carry

    lax.fori_loop(0, rows // TILE, finish, 0)

    lax.fori_loop(groups - LAG - 1, groups, sent_on, 0)


def solution(mesh):
    members = 4
    groups = mesh.shape["depth"] // members

    def shards(volume, shear, footprint):
        slices, rows, columns = volume.shape
        tall = rows + 2 * HALO
        dma = pltpu.SemaphoreType.DMA
        return pl.pallas_call(
            functools.partial(kernel, groups, members),
            out_shape=jax.ShapeDtypeStruct((4, rows, LANES), jnp.float32),
            in_specs=[
                pl.BlockSpec(memory_space=pltpu.HBM),
                pl.BlockSpec(memory_space=pltpu.HBM),
                pl.BlockSpec(memory_space=pltpu.HBM),
            ],
            out_specs=pl.BlockSpec(memory_space=pltpu.VMEM),
            scratch_shapes=[
                pltpu.SMEM(shear.shape, jnp.int32),
                pltpu.SMEM(footprint.shape, jnp.int32),
                pltpu.VMEM((slices + 2, tall, columns + 2 * LANES), jnp.bfloat16),
                pltpu.VMEM((slices, HALO, columns), jnp.bfloat16),
                pltpu.VMEM((slices, HALO, columns), jnp.bfloat16),
                pltpu.VMEM((slices, 2, 2 * WIDE, WIDE), jnp.bfloat16),
                pltpu.VMEM((4, slices, members, rows, LANES), jnp.float32),
                pltpu.VMEM((4, slices, members, rows, LANES), jnp.float32),
                pltpu.VMEM((groups, members, 4, rows, LANES), jnp.bfloat16),
                pltpu.VMEM((groups, members, 4, rows, LANES), jnp.bfloat16),
                pltpu.VMEM((groups, 4, rows, LANES), jnp.bfloat16),
                pltpu.VMEM((groups, 4, rows, LANES), jnp.bfloat16),
                dma,
                dma((2,)),
                dma((2, columns // WIDE)),
                dma((2, columns // WIDE)),
                dma((2, columns // WIDE)),
                dma((2, columns // WIDE)),
                dma((groups, members)),
                dma((groups, members)),
                dma((groups,)),
                dma((groups,)),
                pltpu.SemaphoreType.REGULAR((3, 2)),
            ],
            compiler_params=pltpu.CompilerParams(
                collective_id=0,
                has_side_effects=True,
                vmem_limit_bytes=48 * 2**20,
            ),
        )(*(pltpu.with_memory_space_constraint(a, pltpu.HBM) for a in (shear, footprint, volume)))

    return jax.shard_map(
        shards,
        mesh=mesh,
        in_specs=(P("depth", "tile", None), P(), P("depth", None)),
        out_specs=P(None, "tile", "depth"),
        check_vma=False,
    )
```
